512 devices in a mesh: dp: 32 (over z_lo, y, core), blk: 16 (over z_hi, x).
Axes of the slice: x: 4, y: 8, z: 8 (z_hi: 4, z_lo: 2; z = z_hi * 2 + z_lo), core: 2. Of those that a mesh axis runs over, the one named last changes fastest.
Arguments:
- hidden_in: bfloat16 [12288, 1152], P(('dp', 'blk')), may hold values from -6 to 6
- gain_mlp: float32 [1152], replicated, may hold values from 0.1 to 1.9
- gain_final: float32 [1152], replicated, may hold values from 0.1 to 1.9
- w_in: bfloat16 [1152, 4304], P(None, 'blk'), may hold values from -0.1875 to 0.1875
- w_out: bfloat16 [4304, 1152], P('blk'), may hold values from -0.09375 to 0.09375
- image_embeds: bfloat16 [12288, 1152], P(('dp', 'blk')), may hold values from -6 to 6
- pair_ids: int32 [12288], P(('dp', 'blk')), may hold values from 0 to 383
- teacher_logits: bfloat16 [32, 384, 384], P('dp', None, 'blk'), may hold values from -12 to 12
Outputs:
- grad_hidden: float32 [12288, 1152], P(('dp', 'blk'))
- grad_w_in: float32 [1152, 4304], P(None, 'blk')
- grad_w_out: float32 [4304, 1152], P('blk')
The draws below stay inside these ranges and needn't reach their ends.
All inputs are finite; a program needn't handle non-finite values.
Results may differ from the reference program's by a relative error of at most 0.0067.
Values may be sent and summed in bfloat16 or wider, within the bound.
No kernel may reach another device: no remote copies, remote signals or barrier semaphores. Data moves between devices by JAX's collectives and lax.ppermute only.
A program may use at most 64 MiB of HBM per device.

```python
import jax
import jax.numpy as jnp
from jax import lax

D = 1152
FF = 4304
G = 384
B = 12288
N_DP = 32


def with_ends(entries, own_key, low, high):
    longest = entries.shape.index(max(entries.shape))
    spots = []
    for shift in (0, 1):
        where = [jax.random.randint(jax.random.fold_in(own_key, axis), (), 0, length) for axis, length in enumerate(entries.shape)]
        where[longest] = (where[longest] + shift) % entries.shape[longest]
        spots.append(tuple(where))
    return entries.at[spots[0]].set(low).at[spots[1]].set(high)


def level_of(stream_key, shape, pieces, smallest, high):
    level, own = 1.0, jax.random.fold_in(stream_key, 6)
    for dim, parts in pieces:
        steps = jnp.exp(jax.random.uniform(jax.random.fold_in(own, dim), (parts,), jnp.float32, smallest / len(pieces), high / len(pieces)))
        level = level * jnp.repeat(steps, shape[dim] // parts).reshape([-1 if axis == dim else 1 for axis in range(len(shape))])
    return level


def bell_draw(rng, extent, width, reach, split=(), dtype=jnp.bfloat16):
    values = jax.random.normal(rng, extent, jnp.float32) * width
    if len(split) > 0:
        values = level_of(rng, extent, split, -0.22, 0.18) * values
    return jnp.clip(values, min=-reach, max=reach).astype(dtype)


def setup_inputs(seed: int = 0) -> dict:
    key_list = jax.random.split(jax.random.key(seed), 9)
    return {
        "hidden_in": bell_draw(key_list[0], (B, D), 1.0, 6.0, ((0, 512),)),
        "gain_mlp": jnp.clip(1.0 + 0.18 * jax.random.normal(key_list[1], (D,), jnp.float32), 0.1, 1.9),
        "gain_final": jnp.clip(1.0 + 0.18 * jax.random.normal(key_list[2], (D,), jnp.float32), 0.1, 1.9),
        "w_in": bell_draw(key_list[3], (D, FF), D ** -0.5, 0.1875, ((1, 16),)),
        "w_out": bell_draw(key_list[4], (FF, D), FF ** -0.5, 0.09375, ((0, 16),)),
        "image_embeds": bell_draw(key_list[5], (B, D), 1.0, 6.0, ((0, 512),)),
        "pair_ids": with_ends(jax.random.randint(key_list[6], (B,), 0, G), jax.random.fold_in(key_list[6], 1), 0, G - 1).astype(jnp.int32),
        "teacher_logits": bell_draw(key_list[7], (N_DP, G, G), 3.0, 12.0, ((0, 32), (2, 16))),
    }


epsilon = 1e-06
logit_scale = 10.0
logit_bias = -2.0
gelu_coeff = 0.7978845608028654

def layer_norm(values, gain_vec):
    row_mean = lax.optimization_barrier(jnp.mean(values, axis=-1, keepdims=True))
    centred = values - row_mean
    variance = lax.optimization_barrier(jnp.mean(centred * centred, axis=-1, keepdims=True))
    inverse = lax.rsqrt(variance + epsilon)
    normed = centred * inverse
    return (normed, inverse, normed * gain_vec)

def norm_backward(grad_normed, normed, inverse):
    mean_grad = lax.optimization_barrier(jnp.mean(grad_normed, axis=-1, keepdims=True))
    mean_cross = lax.optimization_barrier(jnp.mean(grad_normed * normed, axis=-1, keepdims=True))
    return inverse * (grad_normed - mean_grad - normed * mean_cross)

def gelu_both(pre_act):
    inner_arg = gelu_coeff * (pre_act + 0.044715 * pre_act * pre_act * pre_act)
    tangent = jnp.tanh(inner_arg)
    gelu_value = 0.5 * pre_act * (1.0 + tangent)
    gelu_slope = 0.5 * (1.0 + tangent) + 0.5 * pre_act * (1.0 - tangent * tangent) * gelu_coeff * (1.0 + 3.0 * 0.044715 * pre_act * pre_act)
    return (gelu_value, gelu_slope)

def reference(hidden_in, gain_mlp, gain_final, w_in, w_out, image_embeds, pair_ids, teacher_logits):
    hidden = hidden_in.astype(jnp.float32)
    normed_in, inverse_in, scaled_in = layer_norm(hidden, gain_mlp)
    mlp_input = scaled_in.astype(jnp.bfloat16)
    pre_act = jnp.dot(mlp_input, w_in, preferred_element_type=jnp.float32)
    gelu_value, gelu_slope = gelu_both(pre_act)
    activation = gelu_value.astype(jnp.bfloat16)
    residual = hidden + jnp.dot(activation, w_out, preferred_element_type=jnp.float32)
    normed_out, inverse_out, final_out = layer_norm(residual, gain_final)
    length = jnp.sqrt(lax.optimization_barrier(jnp.sum(final_out * final_out, axis=-1, keepdims=True)) + epsilon)
    unit_text = final_out / length
    text_embed = unit_text.astype(jnp.bfloat16)
    image_float = image_embeds.astype(jnp.float32)
    image_unit = (image_float * lax.rsqrt(lax.optimization_barrier(jnp.sum(image_float * image_float, axis=-1, keepdims=True)) + epsilon)).astype(jnp.bfloat16)
    text_groups = text_embed.astype(jnp.float32).reshape(N_DP, G, D)
    image_groups = image_unit.astype(jnp.float32).reshape(N_DP, G, D)
    group_pairs = pair_ids.reshape(N_DP, G)
    logits = jnp.einsum('gid,gjd->gij', image_groups, text_groups) * logit_scale + logit_bias
    same_pair = (group_pairs[:, :, None] == group_pairs[:, None, :]).astype(jnp.float32)
    target = 0.5 * same_pair + 0.5 * jax.nn.sigmoid(teacher_logits.astype(jnp.float32))
    pair_grad = (jax.nn.sigmoid(logits) - target).astype(jnp.bfloat16)
    text_grad = logit_scale * jnp.einsum('gij,gid->gjd', pair_grad.astype(jnp.float32), image_groups)
    text_grad = text_grad.reshape(B, D)
    radial = lax.optimization_barrier(jnp.sum(unit_text * text_grad, axis=-1, keepdims=True))
    grad_final = (text_grad - unit_text * radial) / length
    grad_residual = norm_backward(grad_final * gain_final, normed_out, inverse_out)
    residual_rows = grad_residual.astype(jnp.bfloat16)
    grad_activation = jnp.dot(residual_rows, w_out.T, preferred_element_type=jnp.float32)
    grad_pre = (grad_activation * gelu_slope).astype(jnp.bfloat16)
    grad_w_out = jnp.dot(activation.T, residual_rows, preferred_element_type=jnp.float32)
    grad_w_in = jnp.dot(mlp_input.T, grad_pre, preferred_element_type=jnp.float32)
    grad_input_norm = jnp.dot(grad_pre, w_in.T, preferred_element_type=jnp.float32)
    grad_hidden = grad_residual + norm_backward(grad_input_norm * gain_mlp, normed_in, inverse_in)
    return (grad_hidden, grad_w_in, grad_w_out)
```

```python
import jax
import jax.numpy as jnp
from jax import lax
from jax.sharding import Mesh
from jax.sharding import PartitionSpec as P

epsilon = 1e-06
logit_scale = 10.0
logit_bias = -2.0
gelu_coeff = 0.7978845608028654

DP = ("zl", "y", "co")
BLK = ("zh", "x")
RING = ("zl", "y")
LANES = 128


def layer_norm(values, gain_vec):
    row_mean = jnp.mean(values, axis=-1, keepdims=True)
    centred = values - row_mean
    variance = jnp.mean(centred * centred, axis=-1, keepdims=True)
    inverse = lax.rsqrt(variance + epsilon)
    normed = centred * inverse
    return (normed, inverse, normed * gain_vec)


def norm_backward(grad_normed, normed, inverse):
    mean_grad = jnp.mean(grad_normed, axis=-1, keepdims=True)
    mean_cross = jnp.mean(grad_normed * normed, axis=-1, keepdims=True)
    return inverse * (grad_normed - mean_grad - normed * mean_cross)


def gelu_both(pre_act):
    inner_arg = gelu_coeff * (pre_act + 0.044715 * pre_act * pre_act * pre_act)
    tangent = jnp.tanh(inner_arg)
    gelu_value = 0.5 * pre_act * (1.0 + tangent)
    gelu_slope = 0.5 * (1.0 + tangent) + 0.5 * pre_act * (1.0 - tangent * tangent) * gelu_coeff * (
        1.0 + 3.0 * 0.044715 * pre_act * pre_act
    )
    return (gelu_value, gelu_slope)


def to_all(block, axes):
    count = lax.axis_size(axes)
    copies = jnp.broadcast_to(block[None], (count,) + block.shape)
    return lax.all_to_all(copies, axes, 0, 0)


def pack(grad):
    rows = grad.shape[0]
    width = grad.shape[1]
    blocks = width // LANES
    tall = grad.reshape(rows, blocks, LANES).transpose(1, 0, 2).reshape(rows * blocks, LANES)
    return tall.astype(jnp.bfloat16)


def unpack(tall, rows, width):
    blocks = width // LANES
    grad = tall[: rows * blocks].reshape(blocks, rows, LANES).transpose(1, 0, 2)
    return grad.reshape(rows, width).astype(jnp.float32)


def per_device(
    hidden_in, gain_mlp, gain_final, w_in, w_out, image_embeds, pair_ids, teacher_logits
):
    row_count, width = hidden_in.shape
    units = w_in.shape[1]
    blocks = lax.axis_size(BLK)
    group = row_count * blocks
    hidden = hidden_in.astype(jnp.float32)
    normed_in, inverse_in, scaled_in = layer_norm(hidden, gain_mlp)
    mlp_input = scaled_in.astype(jnp.bfloat16)

    image_float = image_embeds.astype(jnp.float32)
    image_unit = (
        image_float
        * lax.rsqrt(jnp.sum(image_float * image_float, axis=-1, keepdims=True) + epsilon)
    ).astype(jnp.bfloat16)
    id_cols = jnp.stack([pair_ids & 127, pair_ids >> 7], axis=1).astype(jnp.bfloat16)
    payload = jnp.concatenate(
        [image_unit, jnp.pad(id_cols, ((0, 0), (0, LANES - 2)))], axis=1
    )
    with jax.named_scope("img_z"):
        column = to_all(payload, "zh").reshape(-1, width + LANES)

    with jax.named_scope("ag1"):
        group_input = to_all(mlp_input, BLK).reshape(group, width)
    with jax.named_scope("img_x"):
        images = to_all(column, "x").reshape(group, width + LANES)
    pre_act = jnp.dot(group_input, w_in, preferred_element_type=jnp.float32)
    gelu_value, gelu_slope = gelu_both(pre_act)
    activation = gelu_value.astype(jnp.bfloat16)
    part_sum = jnp.dot(activation, w_out, preferred_element_type=jnp.float32).astype(jnp.bfloat16)
    with jax.named_scope("rs1"):
        parts = lax.all_to_all(part_sum.reshape(blocks, row_count, width), BLK, 0, 0)
    residual = hidden + jnp.sum(parts.astype(jnp.float32), axis=0)
    normed_out, inverse_out, final_out = layer_norm(residual, gain_final)
    length = jnp.sqrt(jnp.sum(final_out * final_out, axis=-1, keepdims=True) + epsilon)
    unit_text = final_out / length
    text_embed = unit_text.astype(jnp.bfloat16)

    image_rows = images[:, :width]
    image_low = images[:, width].astype(jnp.int32)
    image_high = images[:, width + 1].astype(jnp.int32)
    image_ids = image_high * 128 + image_low
    teacher = teacher_logits[0].T.reshape(row_count, 4, 4, row_count).transpose(0, 2, 1, 3)
    teacher = teacher.reshape(row_count, group).astype(jnp.float32)
    logits = lax.dot_general(
        text_embed, image_rows, (((1,), (1,)), ((), ())), preferred_element_type=jnp.float32
    )
    logits = logits * logit_scale + logit_bias
    same_pair = (pair_ids[:, None] == image_ids[None, :]).astype(jnp.float32)
    target = 0.5 * same_pair + 0.5 * jax.nn.sigmoid(teacher)
    pair_grad = (jax.nn.sigmoid(logits) - target).astype(jnp.bfloat16)
    text_grad = logit_scale * jnp.dot(pair_grad, image_rows, preferred_element_type=jnp.float32)
    radial = jnp.sum(unit_text * text_grad, axis=-1, keepdims=True)
    grad_final = (text_grad - unit_text * radial) / length
    grad_residual = norm_backward(grad_final * gain_final, normed_out, inverse_out)
    residual_rows = grad_residual.astype(jnp.bfloat16)
    with jax.named_scope("ag2"):
        group_grads = to_all(residual_rows, BLK).reshape(group, width)
    grad_activation = lax.dot_general(
        group_grads, w_out, (((1,), (1,)), ((), ())), preferred_element_type=jnp.float32
    )
    grad_pre = (grad_activation * gelu_slope).astype(jnp.bfloat16)
    part_w_out = lax.dot_general(
        activation, group_grads, (((0,), (0,)), ((), ())), preferred_element_type=jnp.float32
    )
    part_w_in = lax.dot_general(
        grad_pre, group_input, (((0,), (0,)), ((), ())), preferred_element_type=jnp.float32
    )
    part_norm = lax.dot_general(
        grad_pre, w_in, (((1,), (1,)), ((), ())), preferred_element_type=jnp.float32
    ).astype(jnp.bfloat16)

    both = jnp.stack([pack(part_w_out), pack(part_w_in)])
    tall = both.shape[1]
    ring = lax.axis_size(RING)
    chunk = -(-tall // (8 * ring)) * 8
    both = jnp.pad(both, ((0, 0), (0, chunk * ring - tall), (0, 0)))
    with jax.named_scope("rs_co"):
        pair = lax.all_to_all(both, "co", 0, 0)
    mine = (pair[0].astype(jnp.float32) + pair[1].astype(jnp.float32)).astype(jnp.bfloat16)
    with jax.named_scope("rs_dp"):
        slices = lax.all_to_all(mine.reshape(ring, chunk, LANES), RING, 0, 0)
    with jax.named_scope("rs2"):
        norm_parts = lax.all_to_all(part_norm.reshape(blocks, row_count, width), BLK, 0, 0)
    total = jnp.sum(slices.astype(jnp.float32), axis=0).astype(jnp.bfloat16)
    with jax.named_scope("ag_dp"):
        whole = to_all(total, RING).reshape(ring * chunk, LANES)
    with jax.named_scope("ag_co"):
        wholes = to_all(whole, "co")
    grad_w_out = unpack(wholes[0], units, width)
    grad_w_in = unpack(wholes[1], units, width).T

    grad_input_norm = jnp.sum(norm_parts.astype(jnp.float32), axis=0)
    grad_hidden = grad_residual + norm_backward(grad_input_norm * gain_mlp, normed_in, inverse_in)
    return (grad_hidden, grad_w_in, grad_w_out)


def solution(mesh):
    fine = Mesh(mesh.devices.reshape(2, 8, 2, 4, 4), ("zl", "y", "co", "zh", "x"))
    rows = DP + BLK
    in_specs = (
        P(rows, None),
        P(),
        P(),
        P(None, BLK),
        P(BLK, None),
        P(rows, None),
        P(rows),
        P(DP, None, BLK),
    )
    out_specs = (P(rows, None), P(None, BLK), P(BLK, None))
    return jax.shard_map(
        per_device, mesh=fine, in_specs=in_specs, out_specs=out_specs, check_vma=False
    )
```

```python
import jax
import jax.numpy as jnp
from jax import lax
from jax.experimental import pallas as pl
from jax.experimental.pallas import tpu as pltpu
from jax.sharding import Mesh
from jax.sharding import PartitionSpec as P


epsilon = 1e-06
logit_scale = 10.0
logit_bias = -2.0
gelu_coeff = 0.7978845608028654

DP = ("zl", "y", "co")
BLK = ("zh", "x")
RING = ("zl", "y")
LANES = 128
VMEM_GRANT = 8 * 2**20
F32 = jnp.float32
BF16 = jnp.bfloat16

NT = (((1,), (1,)), ((), ()))
TN = (((0,), (0,)), ((), ()))
NN = (((1,), (0,)), ((), ()))


def shape(dims, dtype):
    return jax.ShapeDtypeStruct(dims, dtype)


def call(body, outs, *args, scratch=(), flops=0):
    size = sum(a.size * a.dtype.itemsize for a in args)
    size += sum(o.size * o.dtype.itemsize for o in outs)
    near = pl.BlockSpec(memory_space=pltpu.VMEM)
    return pl.pallas_call(
        body,
        out_shape=tuple(outs),
        in_specs=[near] * len(args),
        out_specs=tuple([near] * len(outs)),
        scratch_shapes=list(scratch),
        compiler_params=pltpu.CompilerParams(vmem_limit_bytes=VMEM_GRANT),
        cost_estimate=pl.CostEstimate(flops=flops, bytes_accessed=size, transcendentals=0),
    )(*args)


def dot(a, b, dims):
    return lax.dot_general(a, b, dims, preferred_element_type=F32)


def norm_parts(values):
    row_mean = jnp.mean(values, axis=-1, keepdims=True)
    centred = values - row_mean
    variance = jnp.mean(centred * centred, axis=-1, keepdims=True)
    inverse = lax.rsqrt(variance + epsilon)
    return centred * inverse, inverse


def norm_backward(grad_normed, normed, inverse):
    mean_grad = jnp.mean(grad_normed, axis=-1, keepdims=True)
    mean_cross = jnp.mean(grad_normed * normed, axis=-1, keepdims=True)
    return inverse * (grad_normed - mean_grad - normed * mean_cross)


def gelu_both(pre_act):
    inner_arg = gelu_coeff * (pre_act + 0.044715 * pre_act * pre_act * pre_act)
    tangent = jnp.tanh(inner_arg)
    gelu_value = 0.5 * pre_act * (1.0 + tangent)
    gelu_slope = 0.5 * (1.0 + tangent) + 0.5 * pre_act * (1.0 - tangent * tangent) * gelu_coeff * (
        1.0 + 3.0 * 0.044715 * pre_act * pre_act
    )
    return gelu_value, gelu_slope


def text_in(hidden_ref, gain_ref, out_ref):
    normed, _ = norm_parts(hidden_ref[...].astype(F32))
    rows = (normed * gain_ref[...]).astype(BF16)
    for k in range(out_ref.shape[0]):
        out_ref[k] = rows


def column_of(row_ref):
    count = row_ref.shape[1]
    spread = jnp.broadcast_to(row_ref[...], (count, count))
    down = lax.broadcasted_iota(jnp.int32, (count, count), 0)
    along = lax.broadcasted_iota(jnp.int32, (count, count), 1)
    return jnp.sum(jnp.where(down == along, spread, 0), axis=1, keepdims=True)


def image_in(image_ref, id_ref, out_ref):
    image = image_ref[...].astype(F32)
    width = image.shape[1]
    scale = lax.rsqrt(jnp.sum(image * image, axis=-1, keepdims=True) + epsilon)
    out_ref[:, :width] = (image * scale).astype(BF16)
    ids = column_of(id_ref)
    lane = lax.broadcasted_iota(jnp.int32, (image.shape[0], LANES), 1)
    low = jnp.where(lane == 0, ids & 127, 0)
    high = jnp.where(lane == 1, ids >> 7, 0)
    out_ref[:, width:] = (low + high).astype(F32).astype(BF16)


def image_column(p0, p1, p2, p3, out_ref):
    at = lax.axis_index("zh")
    for k, piece in enumerate((p0, p1, p2, p3)):
        out_ref[lax.rem(at + 4 - k, 4)] = piece[...]


def image_all(q0, q1, q2, q3, teacher_ref, id_ref, image_ref, target_ref, tags):
    at = lax.axis_index("x")
    width = image_ref.shape[2]
    rows = image_ref.shape[1]
    for k, piece in enumerate((q0, q1, q2, q3)):
        x = lax.rem(at + 4 - k, 4)
        for z in range(4):
            image_ref[z * 4 + x] = piece[z, :, :width]
            tags[z * 4 + x] = piece[z, :, width:].astype(F32)
    marks = tags[...].reshape(16 * rows, LANES).astype(BF16)
    row = lax.broadcasted_iota(jnp.int32, (8, LANES), 0)
    lane = lax.broadcasted_iota(jnp.int32, (8, LANES), 1)
    pick = jnp.where(row == lane, 1.0, 0.0).astype(BF16)
    ids = dot(pick, marks, NT)
    image_id = ids[0:1] + 128.0 * ids[1:2]
    text_id = column_of(id_ref).astype(F32)
    same = jnp.where(text_id == image_id, 0.5, 0.0)
    target_ref[...] = same + 0.5 * jax.nn.sigmoid(teacher_ref[...].astype(F32))


def forward(rows_ref, w_in_ref, w_out_ref, part_ref, act_ref, slope_ref):
    blocks, rows, width = part_ref.shape
    pre_act = dot(rows_ref[...].reshape(blocks * rows, width), w_in_ref[...], NT)
    value, slope = gelu_both(pre_act)
    act = value.astype(BF16)
    act_ref[...] = act
    slope_ref[...] = slope
    part_ref[...] = dot(act, w_out_ref[...], NN).astype(BF16).reshape(blocks, rows, width)


def middle(part_ref, hidden_ref, gain_ref, image_ref, target_ref, out_ref, grad_ref):
    blocks, rows, width = part_ref.shape
    total = part_ref[0].astype(F32)
    for k in range(1, blocks):
        total = total + part_ref[k].astype(F32)
    residual = hidden_ref[...].astype(F32) + total
    gain = gain_ref[...]
    normed, inverse = norm_parts(residual)
    final = normed * gain
    length = jnp.sqrt(jnp.sum(final * final, axis=-1, keepdims=True) + epsilon)
    unit = final / length
    images = image_ref[...].reshape(blocks * rows, width)
    logits = dot(unit.astype(BF16), images, NT) * logit_scale + logit_bias
    pair_grad = (jax.nn.sigmoid(logits) - target_ref[...]).astype(BF16)
    text_grad = logit_scale * dot(pair_grad, images, NN)
    radial = jnp.sum(unit * text_grad, axis=-1, keepdims=True)
    grad_final = (text_grad - unit * radial) / length
    grad = norm_backward(grad_final * gain, normed, inverse)
    grad_ref[...] = grad
    sent = grad.astype(BF16)
    for k in range(blocks):
        out_ref[k] = sent


def backward(rows_ref, w_out_ref, slope_ref, grad_ref):
    blocks, rows, width = rows_ref.shape
    grad_act = dot(rows_ref[...].reshape(blocks * rows, width), w_out_ref[...], NT)
    grad_ref[...] = (grad_act * slope_ref[...]).astype(BF16)


def input_grad(grad_ref, w_in_ref, k0, k1, k2, k3, held):
    at = lax.axis_index("x")
    held[...] = dot(grad_ref[...], w_in_ref[...], NN).astype(BF16).reshape(held.shape)
    for k, out in enumerate((k0, k1, k2, k3)):
        x = lax.rem(at + k, 4)
        for z in range(4):
            out[z] = held[z * 4 + x]


def packed(a_ref, b_ref, out_ref, units, step, width):
    a = a_ref[...]
    b = b_ref[...]
    b = b.reshape(a.shape[0], width)
    for c in range(width // LANES):
        tile = dot(a, b[:, c * LANES : (c + 1) * LANES], TN)
        out_ref[pl.ds(c * step, units), :] = tile.astype(out_ref.dtype)


def weight_grad(first, step, act_ref, grads_ref, pre_ref, rows_ref, out_ref):
    units = act_ref.shape[1]
    width = grads_ref.shape[2]
    core = lax.axis_index("co")
    out_ref[...] = jnp.zeros_like(out_ref)

    @pl.when(core == first)
    def _():
        packed(act_ref, grads_ref, out_ref, units, step, width)

    @pl.when(core != first)
    def _():
        packed(pre_ref, rows_ref, out_ref, units, step, width)


def join(kept_ref, got_ref, out_ref):
    ring, chunk, lanes = out_ref.shape
    total = kept_ref[...] + got_ref[...].astype(F32)
    out_ref[...] = total.astype(BF16).reshape(ring, chunk, lanes)


def ring_sum(slices_ref, out_ref):
    total = slices_ref[0].astype(F32)
    for k in range(1, slices_ref.shape[0]):
        total = total + slices_ref[k].astype(F32)
    sent = total.astype(BF16)
    for k in range(out_ref.shape[0]):
        out_ref[k] = sent


def unpack(step, mine_ref, other_ref, w_out_ref, w_in_ref):
    units, width = w_out_ref.shape
    core = lax.axis_index("co")

    def spread(src, dst):
        for c in range(width // LANES):
            dst[:, c * LANES : (c + 1) * LANES] = src[pl.ds(c * step, units), :].astype(F32)

    @pl.when(core == 0)
    def _():
        spread(mine_ref, w_out_ref)
        spread(other_ref, w_in_ref)

    @pl.when(core != 0)
    def _():
        spread(other_ref, w_out_ref)
        spread(mine_ref, w_in_ref)


def column_sum(k0, k1, k2, k3, keep_ref, s1, s2, s3, held):
    at = lax.axis_index("zh")
    total = k0[...].astype(F32) + k1[...].astype(F32)
    held[...] = total + k2[...].astype(F32) + k3[...].astype(F32)
    keep_ref[...] = held[at]
    for k, out in enumerate((s1, s2, s3)):
        out[...] = held[lax.rem(at + k + 1, 4)].astype(BF16)


def last(keep_ref, g1, g2, g3, hidden_ref, gain_ref, grad_ref, out_ref):
    total = keep_ref[...] + g1[...].astype(F32) + g2[...].astype(F32) + g3[...].astype(F32)
    normed, inverse = norm_parts(hidden_ref[...].astype(F32))
    out_ref[...] = grad_ref[...] + norm_backward(total * gain_ref[...], normed, inverse)


def shift(value, axis, by):
    length = lax.axis_size(axis)
    return lax.ppermute(value, axis, [(i, (i + by) % length) for i in range(length)])


def per_device(
    hidden_in, gain_mlp, gain_final, w_in, w_out, image_embeds, pair_ids, teacher_logits
):
    rows, width = hidden_in.shape
    units = w_in.shape[1]
    blocks = lax.axis_size(BLK)
    ring = lax.axis_size(RING)
    group = rows * blocks
    gain_mlp = gain_mlp.reshape(1, width)
    gain_final = gain_final.reshape(1, width)
    ids = pair_ids.reshape(1, rows)
    w_in_rows = w_in.T
    teacher = teacher_logits[0].T
    spread = shape((blocks, rows, width), BF16)
    matmul = 2 * group * units * width

    (copies,) = call(text_in, [spread], hidden_in, gain_mlp)
    group_input = lax.all_to_all(copies, BLK, 0, 0)

    (payload,) = call(image_in, [shape((rows, width + LANES), BF16)], image_embeds, ids)
    near = [shift(payload, "zh", k) for k in (1, 2, 3)]
    (column,) = call(image_column, [shape((4, rows, width + LANES), BF16)], payload, *near)
    far = [shift(column, "x", k) for k in (1, 2, 3)]
    images, target = call(
        image_all,
        [spread, shape((rows, group), F32)],
        column,
        *far,
        teacher,
        ids,
        scratch=[pltpu.VMEM((blocks, rows, LANES), F32)],
    )

    part, act, slope = call(
        forward,
        [spread, shape((group, units), BF16), shape((group, units), F32)],
        group_input,
        w_in_rows,
        w_out,
        flops=2 * matmul,
    )
    parts = lax.all_to_all(part, BLK, 0, 0)
    copies, grad_residual = call(
        middle, [spread, shape((rows, width), F32)], parts, hidden_in, gain_final, images, target
    )
    group_grads = lax.all_to_all(copies, BLK, 0, 0)
    (grad_pre,) = call(
        backward, [shape((group, units), BF16)], group_grads, w_out, slope, flops=matmul
    )

    step = -(-units // 16) * 16
    chunk = -(-(step * (width // LANES)) // (8 * ring)) * 8
    tall = chunk * ring

    def grads(first, dtype):
        return call(
            lambda *refs: weight_grad(first, step, *refs),
            [shape((tall, LANES), dtype)],
            act,
            group_grads,
            grad_pre,
            group_input,
            flops=matmul,
        )[0]

    give = grads(1, BF16)
    got = shift(give, "co", 1)
    keep = grads(0, F32)
    (mine,) = call(join, [shape((ring, chunk, LANES), BF16)], keep, got)
    slices = lax.all_to_all(mine, RING, 0, 0)

    quarter = shape((4, rows, width), BF16)
    k0, s1, s2, s3 = call(
        input_grad,
        [quarter] * 4,
        grad_pre,
        w_in_rows,
        flops=matmul,
        scratch=[pltpu.VMEM((blocks, rows, width), BF16)],
    )
    arrived = [shift(s, "x", k + 1) for k, s in enumerate((s1, s2, s3))]
    own, s1, s2, s3 = call(
        column_sum,
        [shape((rows, width), F32)] + [shape((rows, width), BF16)] * 3,
        k0,
        *arrived,
        scratch=[pltpu.VMEM((4, rows, width), F32)],
    )
    arrived = [shift(s, "zh", k + 1) for k, s in enumerate((s1, s2, s3))]
    (grad_hidden,) = call(
        last, [shape((rows, width), F32)], own, *arrived, hidden_in, gain_mlp, grad_residual
    )

    (copies,) = call(ring_sum, [shape((ring, chunk, LANES), BF16)], slices)
    whole = lax.all_to_all(copies, RING, 0, 0).reshape(tall, LANES)
    other = shift(whole, "co", 1)
    grad_w_out, grad_w_in = call(
        lambda *refs: unpack(step, *refs), [shape((units, width), F32)] * 2, whole, other
    )
    return (grad_hidden, grad_w_in.T, grad_w_out)


def solution(mesh):
    fine = Mesh(mesh.devices.reshape(2, 8, 2, 4, 4), ("zl", "y", "co", "zh", "x"))
    every = DP + BLK
    in_specs = (
        P(every, None),
        P(),
        P(),
        P(None, BLK),
        P(BLK, None),
        P(every, None),
        P(every),
        P(DP, None, BLK),
    )
    out_specs = (P(every, None), P(None, BLK), P(BLK, None))
    return jax.shard_map(
        per_device, mesh=fine, in_specs=in_specs, out_specs=out_specs, check_vma=False
    )
```

```python
import jax
import jax.numpy as jnp
from jax import lax
from jax.experimental import pallas as pl
from jax.experimental.pallas import tpu as pltpu
from jax.sharding import Mesh
from jax.sharding import PartitionSpec as P


epsilon = 1e-06
logit_scale = 10.0
logit_bias = -2.0
gelu_coeff = 0.7978845608028654

DP = ("zl", "y", "co")
BLK = ("zh", "x")
RING = ("zl", "y")
LANES = 128
VMEM_GRANT = 8 * 2**20
F32 = jnp.float32
BF16 = jnp.bfloat16

NT = (((1,), (1,)), ((), ()))
TN = (((0,), (0,)), ((), ()))
NN = (((1,), (0,)), ((), ()))


def shape(dims, dtype):
    return jax.ShapeDtypeStruct(dims, dtype)


def call(body, outs, *args, scratch=(), flops=0, grant=VMEM_GRANT):
    size = sum(a.size * a.dtype.itemsize for a in args)
    size += sum(o.size * o.dtype.itemsize for o in outs)
    near = pl.BlockSpec(memory_space=pltpu.VMEM)
    return pl.pallas_call(
        body,
        out_shape=tuple(outs),
        in_specs=[near] * len(args),
        out_specs=tuple([near] * len(outs)),
        scratch_shapes=list(scratch),
        compiler_params=pltpu.CompilerParams(vmem_limit_bytes=grant),
        cost_estimate=pl.CostEstimate(flops=flops, bytes_accessed=size, transcendentals=0),
    )(*args)


def dot(a, b, dims):
    return lax.dot_general(a, b, dims, preferred_element_type=F32)


def norm_parts(values):
    row_mean = jnp.mean(values, axis=-1, keepdims=True)
    centred = values - row_mean
    variance = jnp.mean(centred * centred, axis=-1, keepdims=True)
    inverse = lax.rsqrt(variance + epsilon)
    return centred * inverse, inverse


def norm_backward(grad_normed, normed, inverse):
    mean_grad = jnp.mean(grad_normed, axis=-1, keepdims=True)
    mean_cross = jnp.mean(grad_normed * normed, axis=-1, keepdims=True)
    return inverse * (grad_normed - mean_grad - normed * mean_cross)


def gelu_both(pre_act):
    inner_arg = gelu_coeff * (pre_act + 0.044715 * pre_act * pre_act * pre_act)
    tangent = jnp.tanh(inner_arg)
    gelu_value = 0.5 * pre_act * (1.0 + tangent)
    gelu_slope = 0.5 * (1.0 + tangent) + 0.5 * pre_act * (1.0 - tangent * tangent) * gelu_coeff * (
        1.0 + 3.0 * 0.044715 * pre_act * pre_act
    )
    return gelu_value, gelu_slope


def text_in(hidden_ref, gain_ref, out_ref):
    normed, _ = norm_parts(hidden_ref[...].astype(F32))
    rows = (normed * gain_ref[...].reshape(1, -1)).astype(BF16)
    for k in range(out_ref.shape[0]):
        out_ref[k] = rows


def column_of(row_ref):
    count = row_ref.shape[1]
    spread = jnp.broadcast_to(row_ref[...], (count, count))
    down = lax.broadcasted_iota(jnp.int32, (count, count), 0)
    along = lax.broadcasted_iota(jnp.int32, (count, count), 1)
    return jnp.sum(jnp.where(down == along, spread, 0), axis=1, keepdims=True)


def image_in(image_ref, id_ref, out_ref):
    image = image_ref[...].astype(F32)
    width = image.shape[1]
    scale = lax.rsqrt(jnp.sum(image * image, axis=-1, keepdims=True) + epsilon)
    out_ref[:, :width] = (image * scale).astype(BF16)
    ids = column_of(id_ref)
    lane = lax.broadcasted_iota(jnp.int32, (image.shape[0], LANES), 1)
    low = jnp.where(lane == 0, ids & 127, 0)
    high = jnp.where(lane == 1, ids >> 7, 0)
    out_ref[:, width:] = (low + high).astype(F32).astype(BF16)


def targets(image_ref, teacher_ref, id_ref, target_ref):
    sides, _, rows, deep = image_ref.shape
    group = sides * sides * rows
    marks = image_ref[:, :, :, deep - LANES :].reshape(group, LANES)
    row = lax.broadcasted_iota(jnp.int32, (8, LANES), 0)
    lane = lax.broadcasted_iota(jnp.int32, (8, LANES), 1)
    pick = jnp.where(row == lane, 1.0, 0.0).astype(BF16)
    ids = dot(pick, marks, NT)
    image_id = ids[0:1] + 128.0 * ids[1:2]
    text_id = column_of(id_ref).astype(F32)
    same = jnp.where(text_id == image_id, 0.5, 0.0)
    down = lax.broadcasted_iota(jnp.int32, (group, group), 0)
    along = lax.broadcasted_iota(jnp.int32, (1, group), 1)
    block = along // rows
    wanted = (lax.rem(block, sides) * sides + block // sides) * rows + lax.rem(along, rows)
    order = jnp.where(down == wanted, 1.0, 0.0).astype(BF16)
    teacher = dot(teacher_ref[...], order, NN)
    target_ref[...] = same + 0.5 * jax.nn.sigmoid(teacher)


def forward(rows_ref, w_in_ref, w_out_ref, part_ref, act_ref, slope_ref):
    blocks, rows, width = part_ref.shape
    pre_act = dot(rows_ref[...].reshape(blocks * rows, width), w_in_ref[...], NT)
    value, slope = gelu_both(pre_act)
    act = value.astype(BF16)
    act_ref[...] = act
    slope_ref[...] = slope
    part_ref[...] = dot(act, w_out_ref[...], NN).astype(BF16).reshape(blocks, rows, width)


def middle(part_ref, hidden_ref, gain_ref, image_ref, target_ref, out_ref, grad_ref):
    blocks, rows, width = part_ref.shape
    total = part_ref[0].astype(F32)
    for k in range(1, blocks):
        total = total + part_ref[k].astype(F32)
    residual = hidden_ref[...].astype(F32) + total
    gain = gain_ref[...].reshape(1, width)
    normed, inverse = norm_parts(residual)
    final = normed * gain
    length = jnp.sqrt(jnp.sum(final * final, axis=-1, keepdims=True) + epsilon)
    unit = final / length
    images = image_ref[:, :, :, :width].reshape(blocks * rows, width)
    logits = dot(unit.astype(BF16), images, NT) * logit_scale + logit_bias
    pair_grad = (jax.nn.sigmoid(logits) - target_ref[...]).astype(BF16)
    text_grad = logit_scale * dot(pair_grad, images, NN)
    radial = jnp.sum(unit * text_grad, axis=-1, keepdims=True)
    grad_final = (text_grad - unit * radial) / length
    grad = norm_backward(grad_final * gain, normed, inverse)
    grad_ref[...] = grad
    sent = grad.astype(BF16)
    for k in range(blocks):
        out_ref[k] = sent


def backward(rows_ref, w_out_ref, slope_ref, grad_ref):
    blocks, rows, width = rows_ref.shape
    grad_act = dot(rows_ref[...].reshape(blocks * rows, width), w_out_ref[...], NT)
    grad_ref[...] = (grad_act * slope_ref[...]).astype(BF16)


def input_grad(grad_ref, w_in_ref, k0, k1, k2, k3, held):
    at = lax.axis_index("x")
    held[...] = dot(grad_ref[...], w_in_ref[...], NN).astype(BF16).reshape(held.shape)
    for k, out in enumerate((k0, k1, k2, k3)):
        x = lax.rem(at + k, 4)
        for z in range(4):
            out[z] = held[z * 4 + x]


def packed(a_ref, b_ref, out_ref, units, step, width):
    a = a_ref[...]
    b = b_ref[...]
    b = b.reshape(a.shape[0], width)
    for c in range(width // LANES):
        tile = dot(a, b[:, c * LANES : (c + 1) * LANES], TN)
        out_ref[pl.ds(c * step, units), :] = tile.astype(out_ref.dtype)


def weight_grad(first, step, act_ref, grads_ref, pre_ref, rows_ref, out_ref):
    units = act_ref.shape[1]
    width = grads_ref.shape[2]
    core = lax.axis_index("co")
    out_ref[...] = jnp.zeros_like(out_ref)

    @pl.when(core == first)
    def _():
        packed(act_ref, grads_ref, out_ref, units, step, width)

    @pl.when(core != first)
    def _():
        packed(pre_ref, rows_ref, out_ref, units, step, width)


def join(kept_ref, got_ref, out_ref):
    ring, chunk, lanes = out_ref.shape
    total = kept_ref[...] + got_ref[...].astype(F32)
    out_ref[...] = total.astype(BF16).reshape(ring, chunk, lanes)


def ring_sum(slices_ref, out_ref):
    total = slices_ref[0].astype(F32)
    for k in range(1, slices_ref.shape[0]):
        total = total + slices_ref[k].astype(F32)
    sent = total.astype(BF16)
    for k in range(out_ref.shape[0]):
        out_ref[k] = sent


def unpack(step, mine_ref, other_ref, w_out_ref, w_in_ref):
    units, width = w_out_ref.shape
    core = lax.axis_index("co")

    def spread(src, dst):
        for c in range(width // LANES):
            dst[:, c * LANES : (c + 1) * LANES] = src[pl.ds(c * step, units), :].astype(F32)

    @pl.when(core == 0)
    def _():
        spread(mine_ref, w_out_ref)
        spread(other_ref, w_in_ref)

    @pl.when(core != 0)
    def _():
        spread(other_ref, w_out_ref)
        spread(mine_ref, w_in_ref)


def column_sum(k0, k1, k2, k3, keep_ref, s1, s2, s3, held):
    at = lax.axis_index("zh")
    total = k0[...].astype(F32) + k1[...].astype(F32)
    held[...] = total + k2[...].astype(F32) + k3[...].astype(F32)
    keep_ref[...] = held[at]
    for k, out in enumerate((s1, s2, s3)):
        out[...] = held[lax.rem(at + k + 1, 4)].astype(BF16)


def last(keep_ref, g1, g2, g3, hidden_ref, gain_ref, grad_ref, out_ref):
    total = keep_ref[...] + g1[...].astype(F32) + g2[...].astype(F32) + g3[...].astype(F32)
    normed, inverse = norm_parts(hidden_ref[...].astype(F32))
    out_ref[...] = grad_ref[...] + norm_backward(total * gain_ref[...].reshape(1, -1), normed, inverse)


def shift(value, axis, by):
    length = lax.axis_size(axis)
    return lax.ppermute(value, axis, [(i, (i + by) % length) for i in range(length)])


def per_device(
    hidden_in, gain_mlp, gain_final, w_in, w_out, image_embeds, pair_ids, teacher_logits
):
    rows, width = hidden_in.shape
    units = w_in.shape[1]
    blocks = lax.axis_size(BLK)
    ring = lax.axis_size(RING)
    group = rows * blocks
    ids = pair_ids.reshape(1, rows)
    w_in_rows = w_in.T
    teacher = teacher_logits[0].T
    spread = shape((blocks, rows, width), BF16)
    matmul = 2 * group * units * width

    (copies,) = call(text_in, [spread], hidden_in, gain_mlp)
    group_input = lax.all_to_all(copies, BLK, 0, 0)

    (payload,) = call(image_in, [shape((rows, width + LANES), BF16)], image_embeds, ids)
    column = lax.all_gather(payload, "zh")

    part, act, slope = call(
        forward,
        [spread, shape((group, units), BF16), shape((group, units), F32)],
        group_input,
        w_in_rows,
        w_out,
        flops=2 * matmul,
    )
    part, column = lax.optimization_barrier((part, column))
    images = lax.all_gather(column, "x")
    (target,) = call(targets, [shape((rows, group), F32)], images, teacher, ids)
    parts = lax.all_to_all(part, BLK, 0, 0)
    copies, grad_residual = call(
        middle, [spread, shape((rows, width), F32)], parts, hidden_in, gain_final, images, target
    )
    group_grads = lax.all_to_all(copies, BLK, 0, 0)
    (grad_pre,) = call(
        backward, [shape((group, units), BF16)], group_grads, w_out, slope, flops=matmul
    )

    step = -(-units // 16) * 16
    chunk = -(-(step * (width // LANES)) // (8 * ring)) * 8
    tall = chunk * ring

    def grads(first, dtype):
        return call(
            lambda *refs: weight_grad(first, step, *refs),
            [shape((tall, LANES), dtype)],
            act,
            group_grads,
            grad_pre,
            group_input,
            flops=matmul,
        )[0]

    give = grads(1, BF16)
    got = shift(give, "co", 1)
    keep = grads(0, F32)
    (mine,) = call(join, [shape((ring, chunk, LANES), BF16)], keep, got)
    slices = lax.all_to_all(mine, RING, 0, 0)

    quarter = shape((4, rows, width), BF16)
    k0, s1, s2, s3 = call(
        input_grad,
        [quarter] * 4,
        grad_pre,
        w_in_rows,
        flops=matmul,
        scratch=[pltpu.VMEM((blocks, rows, width), BF16)],
    )
    arrived = [shift(s, "x", k + 1) for k, s in enumerate((s1, s2, s3))]
    own, s1, s2, s3 = call(
        column_sum,
        [shape((rows, width), F32)] + [shape((rows, width), BF16)] * 3,
        k0,
        *arrived,
        scratch=[pltpu.VMEM((4, rows, width), F32)],
    )
    arrived = [shift(s, "zh", k + 1) for k, s in enumerate((s1, s2, s3))]
    (grad_hidden,) = call(
        last, [shape((rows, width), F32)], own, *arrived, hidden_in, gain_mlp, grad_residual
    )

    (copies,) = call(ring_sum, [shape((ring, chunk, LANES), BF16)], slices)
    whole = lax.all_to_all(copies, RING, 0, 0).reshape(tall, LANES)
    other = shift(whole, "co", 1)
    grad_w_out, grad_w_in = call(
        lambda *refs: unpack(step, *refs), [shape((units, width), F32)] * 2, whole, other
    )
    return (grad_hidden, grad_w_in.T, grad_w_out)


def solution(mesh):
    fine = Mesh(mesh.devices.reshape(2, 8, 2, 4, 4), ("zl", "y", "co", "zh", "x"))
    every = DP + BLK
    in_specs = (
        P(every, None),
        P(),
        P(),
        P(None, BLK),
        P(BLK, None),
        P(every, None),
        P(every),
        P(DP, None, BLK),
    )
    out_specs = (P(every, None), P(None, BLK), P(BLK, None))
    return jax.shard_map(
        per_device, mesh=fine, in_specs=in_specs, out_specs=out_specs, check_vma=False
    )
```

```python
import jax
import jax.numpy as jnp
from jax import lax
from jax.experimental import pallas as pl
from jax.experimental.pallas import tpu as pltpu
from jax.sharding import Mesh
from jax.sharding import PartitionSpec as P


epsilon = 1e-06
logit_scale = 10.0
logit_bias = -2.0
gelu_coeff = 0.7978845608028654

DP = ("zl", "y", "co")
BLK = ("zh", "x")
RING = ("zl", "y")
LANES = 128
VMEM_GRANT = 8 * 2**20
WHOLE_GRANT = 60 * 2**20
F32 = jnp.float32
BF16 = jnp.bfloat16

NT = (((1,), (1,)), ((), ()))
TN = (((0,), (0,)), ((), ()))
NN = (((1,), (0,)), ((), ()))


def shape(dims, dtype):
    return jax.ShapeDtypeStruct(dims, dtype)


def call(body, outs, *args, far_in=(), scratch=(), flops=0, grant=VMEM_GRANT):
    size = sum(a.size * a.dtype.itemsize for a in args)
    size += sum(o.size * o.dtype.itemsize for o in outs)
    near = pl.BlockSpec(memory_space=pltpu.VMEM)
    far = pl.BlockSpec(memory_space=pl.ANY)
    return pl.pallas_call(
        body,
        out_shape=tuple(outs),
        in_specs=[far if k in far_in else near for k in range(len(args))],
        out_specs=tuple([near] * len(outs)),
        scratch_shapes=list(scratch),
        compiler_params=pltpu.CompilerParams(vmem_limit_bytes=grant),
        cost_estimate=pl.CostEstimate(flops=flops, bytes_accessed=size, transcendentals=0),
    )(*args)


def dot(a, b, dims):
    return lax.dot_general(a, b, dims, preferred_element_type=F32)


def norm_parts(values):
    row_mean = jnp.mean(values, axis=-1, keepdims=True)
    centred = values - row_mean
    variance = jnp.mean(centred * centred, axis=-1, keepdims=True)
    inverse = lax.rsqrt(variance + epsilon)
    return centred * inverse, inverse


def norm_backward(grad_normed, normed, inverse):
    mean_grad = jnp.mean(grad_normed, axis=-1, keepdims=True)
    mean_cross = jnp.mean(grad_normed * normed, axis=-1, keepdims=True)
    return inverse * (grad_normed - mean_grad - normed * mean_cross)


def gelu_both(pre_act):
    inner_arg = gelu_coeff * (pre_act + 0.044715 * pre_act * pre_act * pre_act)
    tangent = jnp.tanh(inner_arg)
    gelu_value = 0.5 * pre_act * (1.0 + tangent)
    gelu_slope = 0.5 * (1.0 + tangent) + 0.5 * pre_act * (1.0 - tangent * tangent) * gelu_coeff * (
        1.0 + 3.0 * 0.044715 * pre_act * pre_act
    )
    return gelu_value, gelu_slope


def column_of(row_ref):
    count = row_ref.shape[1]
    spread = jnp.broadcast_to(row_ref[...], (count, count))
    down = lax.broadcasted_iota(jnp.int32, (count, count), 0)
    along = lax.broadcasted_iota(jnp.int32, (count, count), 1)
    return jnp.sum(jnp.where(down == along, spread, 0), axis=1, keepdims=True)


def prepare(
    hidden_hbm, gain_hbm, image_hbm, id_hbm, out_ref, hidden_ref, gain_ref, image_ref, id_ref, sems
):
    width = hidden_ref.shape[1]
    arrays = ((hidden_hbm, hidden_ref), (gain_hbm, gain_ref), (image_hbm, image_ref), (id_hbm, id_ref))
    moves = [pltpu.make_async_copy(src, dst, sems.at[k]) for k, (src, dst) in enumerate(arrays)]
    for move in moves:
        move.start()
    for move in moves:
        move.wait()
    normed, _ = norm_parts(hidden_ref[...].astype(F32))
    out_ref[:, :width] = (normed * gain_ref[...].reshape(1, width)).astype(BF16)
    image = image_ref[...].astype(F32)
    scale = lax.rsqrt(jnp.sum(image * image, axis=-1, keepdims=True) + epsilon)
    out_ref[:, width : 2 * width] = (image * scale).astype(BF16)
    ids = column_of(id_ref)
    lane = lax.broadcasted_iota(jnp.int32, (image.shape[0], LANES), 1)
    low = jnp.where(lane == 0, ids & 127, 0)
    high = jnp.where(lane == 1, ids >> 7, 0)
    out_ref[:, 2 * width :] = (low + high).astype(F32).astype(BF16)


def split(both_ref, rows_ref, image_ref):
    width = rows_ref.shape[2]
    rows_ref[...] = both_ref[:, :, :width]
    image_ref[...] = both_ref[:, :, width:]


def targets(image_ref, teacher_ref, id_ref, target_ref):
    sides, _, rows, deep = image_ref.shape
    group = sides * sides * rows
    marks = image_ref[:, :, :, deep - LANES :].reshape(group, LANES)
    row = lax.broadcasted_iota(jnp.int32, (8, LANES), 0)
    lane = lax.broadcasted_iota(jnp.int32, (8, LANES), 1)
    pick = jnp.where(row == lane, 1.0, 0.0).astype(BF16)
    ids = dot(pick, marks, NT)
    image_id = ids[0:1] + 128.0 * ids[1:2]
    text_id = column_of(id_ref).astype(F32)
    same = jnp.where(text_id == image_id, 0.5, 0.0)
    down = lax.broadcasted_iota(jnp.int32, (group, group), 0)
    along = lax.broadcasted_iota(jnp.int32, (1, group), 1)
    block = along // rows
    wanted = (lax.rem(block, sides) * sides + block // sides) * rows + lax.rem(along, rows)
    order = jnp.where(down == wanted, 1.0, 0.0).astype(BF16)
    teacher = dot(teacher_ref[...], order, NN)
    target_ref[...] = same + 0.5 * jax.nn.sigmoid(teacher)


def forward(all_ref, w_in_ref, w_out_ref, part_ref, act_ref, slope_ref, rows_ref):
    blocks, rows, width = part_ref.shape
    for x in range(4):
        for z in range(4):
            rows_ref[z * 4 + x] = all_ref[x, z]
    pre_act = dot(rows_ref[...].reshape(blocks * rows, width), w_in_ref[...], NT)
    value, slope = gelu_both(pre_act)
    act = value.astype(BF16)
    act_ref[...] = act
    slope_ref[...] = slope
    part_ref[...] = dot(act, w_out_ref[...], NN).astype(BF16).reshape(blocks, rows, width)


def middle(part_ref, hidden_ref, gain_ref, image_ref, target_ref, out_ref, grad_ref):
    blocks, rows, width = part_ref.shape
    total = part_ref[0].astype(F32)
    for k in range(1, blocks):
        total = total + part_ref[k].astype(F32)
    residual = hidden_ref[...].astype(F32) + total
    gain = gain_ref[...].reshape(1, width)
    normed, inverse = norm_parts(residual)
    final = normed * gain
    length = jnp.sqrt(jnp.sum(final * final, axis=-1, keepdims=True) + epsilon)
    unit = final / length
    images = image_ref[:, :, :, :width].reshape(blocks * rows, width)
    logits = dot(unit.astype(BF16), images, NT) * logit_scale + logit_bias
    pair_grad = (jax.nn.sigmoid(logits) - target_ref[...]).astype(BF16)
    text_grad = logit_scale * dot(pair_grad, images, NN)
    radial = jnp.sum(unit * text_grad, axis=-1, keepdims=True)
    grad_final = (text_grad - unit * radial) / length
    grad = norm_backward(grad_final * gain, normed, inverse)
    grad_ref[...] = grad
    sent = grad.astype(BF16)
    for k in range(blocks):
        out_ref[k] = sent


def backward(rows_ref, w_out_ref, slope_ref, grad_ref):
    blocks, rows, width = rows_ref.shape
    grad_act = dot(rows_ref[...].reshape(blocks * rows, width), w_out_ref[...], NT)
    grad_ref[...] = (grad_act * slope_ref[...]).astype(BF16)


def input_grad(grad_ref, w_in_ref, k0, k1, k2, k3, held):
    at = lax.axis_index("x")
    held[...] = dot(grad_ref[...], w_in_ref[...], NN).astype(BF16).reshape(held.shape)
    for k, out in enumerate((k0, k1, k2, k3)):
        x = lax.rem(at + k, 4)
        for z in range(4):
            out[z] = held[z * 4 + x]


def packed(a_ref, b_ref, out_ref, units, step, width):
    a = a_ref[...]
    b = b_ref[...]
    b = b.reshape(a.shape[0], width)
    for c in range(width // LANES):
        tile = dot(a, b[:, c * LANES : (c + 1) * LANES], TN)
        out_ref[pl.ds(c * step, units), :] = tile.astype(out_ref.dtype)


def weight_grad(first, step, act_ref, grads_ref, pre_ref, rows_ref, out_ref):
    units = act_ref.shape[1]
    width = grads_ref.shape[2]
    core = lax.axis_index("co")
    out_ref[...] = jnp.zeros_like(out_ref)

    @pl.when(core == first)
    def _():
        packed(act_ref, grads_ref, out_ref, units, step, width)

    @pl.when(core != first)
    def _():
        packed(pre_ref, rows_ref, out_ref, units, step, width)


def join(kept_ref, got_ref, out_ref):
    ring, chunk, lanes = out_ref.shape
    total = kept_ref[...] + got_ref[...].astype(F32)
    out_ref[...] = total.astype(BF16).reshape(ring, chunk, lanes)


def ring_sum(slices_ref, out_ref):
    total = slices_ref[0].astype(F32)
    for k in range(1, slices_ref.shape[0]):
        total = total + slices_ref[k].astype(F32)
    sent = total.astype(BF16)
    for k in range(out_ref.shape[0]):
        out_ref[k] = sent


def unpack(step, mine_ref, other_ref, w_out_ref, w_in_ref):
    units, width = w_out_ref.shape
    core = lax.axis_index("co")

    def spread(src, dst):
        for c in range(width // LANES):
            dst[:, c * LANES : (c + 1) * LANES] = src[pl.ds(c * step, units), :].astype(F32)

    @pl.when(core == 0)
    def _():
        spread(mine_ref, w_out_ref)
        spread(other_ref, w_in_ref)

    @pl.when(core != 0)
    def _():
        spread(other_ref, w_out_ref)
        spread(mine_ref, w_in_ref)


def column_sum(k0, k1, k2, k3, keep_ref, s1, s2, s3, held):
    at = lax.axis_index("zh")
    total = k0[...].astype(F32) + k1[...].astype(F32)
    held[...] = total + k2[...].astype(F32) + k3[...].astype(F32)
    keep_ref[...] = held[at]
    for k, out in enumerate((s1, s2, s3)):
        out[...] = held[lax.rem(at + k + 1, 4)].astype(BF16)


def last(keep_ref, g1, g2, g3, hidden_ref, gain_ref, grad_ref, out_ref):
    total = keep_ref[...] + g1[...].astype(F32) + g2[...].astype(F32) + g3[...].astype(F32)
    normed, inverse = norm_parts(hidden_ref[...].astype(F32))
    out_ref[...] = grad_ref[...] + norm_backward(total * gain_ref[...].reshape(1, -1), normed, inverse)


def shift(value, axis, by):
    length = lax.axis_size(axis)
    return lax.ppermute(value, axis, [(i, (i + by) % length) for i in range(length)])


def per_device(
    hidden_in, gain_mlp, gain_final, w_in, w_out, image_embeds, pair_ids, teacher_logits
):
    rows, width = hidden_in.shape
    units = w_in.shape[1]
    blocks = lax.axis_size(BLK)
    ring = lax.axis_size(RING)
    group = rows * blocks
    ids = pair_ids.reshape(1, rows)
    w_in_rows = w_in.T
    teacher = teacher_logits[0].T
    spread = shape((blocks, rows, width), BF16)
    matmul = 2 * group * units * width

    (own_rows,) = call(
        prepare,
        [shape((rows, 2 * width + LANES), BF16)],
        hidden_in,
        gain_mlp,
        image_embeds,
        ids,
        far_in=(0, 1, 2, 3),
        scratch=[
            pltpu.VMEM(hidden_in.shape, BF16),
            pltpu.VMEM(gain_mlp.shape, F32),
            pltpu.VMEM(image_embeds.shape, BF16),
            pltpu.VMEM(ids.shape, ids.dtype),
            pltpu.SemaphoreType.DMA((4,)),
        ],
        grant=WHOLE_GRANT,
    )
    both = lax.all_gather(own_rows, "zh")
    rows_column, column = call(
        split, [shape((4, rows, width), BF16), shape((4, rows, width + LANES), BF16)], both
    )
    everything = lax.all_gather(rows_column, "x")
    part, act, slope, group_input = call(
        forward,
        [spread, shape((group, units), BF16), shape((group, units), F32), spread],
        everything,
        w_in_rows,
        w_out,
        flops=2 * matmul,
    )
    part, column = lax.optimization_barrier((part, column))
    images = lax.all_gather(column, "x")
    (target,) = call(targets, [shape((rows, group), F32)], images, teacher, ids)
    parts = lax.all_to_all(part, BLK, 0, 0)
    copies, grad_residual = call(
        middle, [spread, shape((rows, width), F32)], parts, hidden_in, gain_final, images, target
    )
    group_grads = lax.all_to_all(copies, BLK, 0, 0)
    (grad_pre,) = call(
        backward, [shape((group, units), BF16)], group_grads, w_out, slope, flops=matmul
    )

    step = -(-units // 16) * 16
    chunk = -(-(step * (width // LANES)) // (8 * ring)) * 8
    tall = chunk * ring

    def grads(first, dtype):
        return call(
            lambda *refs: weight_grad(first, step, *refs),
            [shape((tall, LANES), dtype)],
            act,
            group_grads,
            grad_pre,
            group_input,
            flops=matmul,
        )[0]

    give = grads(1, BF16)
    got = shift(give, "co", 1)
    keep = grads(0, F32)
    (mine,) = call(join, [shape((ring, chunk, LANES), BF16)], keep, got)
    slices = lax.all_to_all(mine, RING, 0, 0)

    quarter = shape((4, rows, width), BF16)
    k0, s1, s2, s3 = call(
        input_grad,
        [quarter] * 4,
        grad_pre,
        w_in_rows,
        flops=matmul,
        scratch=[pltpu.VMEM((blocks, rows, width), BF16)],
    )
    arrived = [shift(s, "x", k + 1) for k, s in enumerate((s1, s2, s3))]
    own, s1, s2, s3 = call(
        column_sum,
        [shape((rows, width), F32)] + [shape((rows, width), BF16)] * 3,
        k0,
        *arrived,
        scratch=[pltpu.VMEM((4, rows, width), F32)],
    )
    arrived = [shift(s, "zh", k + 1) for k, s in enumerate((s1, s2, s3))]
    (grad_hidden,) = call(
        last, [shape((rows, width), F32)], own, *arrived, hidden_in, gain_mlp, grad_residual
    )

    (copies,) = call(ring_sum, [shape((ring, chunk, LANES), BF16)], slices)
    whole = lax.all_to_all(copies, RING, 0, 0).reshape(tall, LANES)
    other = shift(whole, "co", 1)
    grad_w_out, grad_w_in = call(
        lambda *refs: unpack(step, *refs), [shape((units, width), F32)] * 2, whole, other
    )
    return (grad_hidden, grad_w_in.T, grad_w_out)


def solution(mesh):
    fine = Mesh(mesh.devices.reshape(2, 8, 2, 4, 4), ("zl", "y", "co", "zh", "x"))
    every = DP + BLK
    in_specs = (
        P(every, None),
        P(),
        P(),
        P(None, BLK),
        P(BLK, None),
        P(every, None),
        P(every),
        P(DP, None, BLK),
    )
    out_specs = (P(every, None), P(None, BLK), P(BLK, None))
    return jax.shard_map(
        per_device, mesh=fine, in_specs=in_specs, out_specs=out_specs, check_vma=False
    )
```

```python
import jax
import jax.numpy as jnp
from jax import lax
from jax.experimental import pallas as pl
from jax.experimental.pallas import tpu as pltpu
from jax.sharding import Mesh
from jax.sharding import PartitionSpec as P


epsilon = 1e-06
logit_scale = 10.0
logit_bias = -2.0
gelu_coeff = 0.7978845608028654

DP = ("zl", "y", "co")
BLK = ("zh", "x")
RING = ("zl", "y")
LANES = 128
VMEM_GRANT = 8 * 2**20
WHOLE_GRANT = 60 * 2**20
F32 = jnp.float32
BF16 = jnp.bfloat16

NT = (((1,), (1,)), ((), ()))
TN = (((0,), (0,)), ((), ()))
NN = (((1,), (0,)), ((), ()))


def shape(dims, dtype):
    return jax.ShapeDtypeStruct(dims, dtype)


def call(body, outs, *args, far_in=(), scratch=(), flops=0, grant=VMEM_GRANT):
    size = sum(a.size * a.dtype.itemsize for a in args)
    size += sum(o.size * o.dtype.itemsize for o in outs)
    near = pl.BlockSpec(memory_space=pltpu.VMEM)
    far = pl.BlockSpec(memory_space=pl.ANY)
    return pl.pallas_call(
        body,
        out_shape=tuple(outs),
        in_specs=[far if k in far_in else near for k in range(len(args))],
        out_specs=tuple([near] * len(outs)),
        scratch_shapes=list(scratch),
        compiler_params=pltpu.CompilerParams(vmem_limit_bytes=grant),
        cost_estimate=pl.CostEstimate(flops=flops, bytes_accessed=size, transcendentals=0),
    )(*args)


def dot(a, b, dims):
    return lax.dot_general(a, b, dims, preferred_element_type=F32)


def norm_parts(values):
    row_mean = jnp.mean(values, axis=-1, keepdims=True)
    centred = values - row_mean
    variance = jnp.mean(centred * centred, axis=-1, keepdims=True)
    inverse = lax.rsqrt(variance + epsilon)
    return centred * inverse, inverse


def norm_backward(grad_normed, normed, inverse):
    mean_grad = jnp.mean(grad_normed, axis=-1, keepdims=True)
    mean_cross = jnp.mean(grad_normed * normed, axis=-1, keepdims=True)
    return inverse * (grad_normed - mean_grad - normed * mean_cross)


def gelu_both(pre_act):
    inner_arg = gelu_coeff * (pre_act + 0.044715 * pre_act * pre_act * pre_act)
    tangent = jnp.tanh(inner_arg)
    gelu_value = 0.5 * pre_act * (1.0 + tangent)
    gelu_slope = 0.5 * (1.0 + tangent) + 0.5 * pre_act * (1.0 - tangent * tangent) * gelu_coeff * (
        1.0 + 3.0 * 0.044715 * pre_act * pre_act
    )
    return gelu_value, gelu_slope


def column_of(row_ref):
    count = row_ref.shape[1]
    spread = jnp.broadcast_to(row_ref[...], (count, count))
    down = lax.broadcasted_iota(jnp.int32, (count, count), 0)
    along = lax.broadcasted_iota(jnp.int32, (count, count), 1)
    return jnp.sum(jnp.where(down == along, spread, 0), axis=1, keepdims=True)


def prepare(
    hidden_hbm, gain_hbm, image_hbm, id_hbm, out_ref, hidden_ref, gain_ref, image_ref, id_ref, sems
):
    width = hidden_ref.shape[1]
    arrays = ((hidden_hbm, hidden_ref), (gain_hbm, gain_ref), (image_hbm, image_ref), (id_hbm, id_ref))
    moves = [pltpu.make_async_copy(src, dst, sems.at[k]) for k, (src, dst) in enumerate(arrays)]
    for move in moves:
        move.start()
    for move in moves:
        move.wait()
    normed, _ = norm_parts(hidden_ref[...].astype(F32))
    out_ref[:, :width] = (normed * gain_ref[...].reshape(1, width)).astype(BF16)
    image = image_ref[...].astype(F32)
    scale = lax.rsqrt(jnp.sum(image * image, axis=-1, keepdims=True) + epsilon)
    out_ref[:, width : 2 * width] = (image * scale).astype(BF16)
    ids = column_of(id_ref)
    lane = lax.broadcasted_iota(jnp.int32, (image.shape[0], LANES), 1)
    low = jnp.where(lane == 0, ids & 127, 0)
    high = jnp.where(lane == 1, ids >> 7, 0)
    out_ref[:, 2 * width :] = (low + high).astype(F32).astype(BF16)


def split(both_ref, rows_ref, image_ref):
    width = rows_ref.shape[2]
    rows_ref[...] = both_ref[:, :, :width]
    image_ref[...] = both_ref[:, :, width:]


def targets(image_ref, teacher_ref, id_ref, target_ref):
    sides, _, rows, deep = image_ref.shape
    group = sides * sides * rows
    marks = image_ref[:, :, :, deep - LANES :].reshape(group, LANES)
    row = lax.broadcasted_iota(jnp.int32, (8, LANES), 0)
    lane = lax.broadcasted_iota(jnp.int32, (8, LANES), 1)
    pick = jnp.where(row == lane, 1.0, 0.0).astype(BF16)
    ids = dot(pick, marks, NT)
    image_id = ids[0:1] + 128.0 * ids[1:2]
    text_id = column_of(id_ref).astype(F32)
    same = jnp.where(text_id == image_id, 0.5, 0.0)
    down = lax.broadcasted_iota(jnp.int32, (group, group), 0)
    along = lax.broadcasted_iota(jnp.int32, (1, group), 1)
    block = along // rows
    wanted = (lax.rem(block, sides) * sides + block // sides) * rows + lax.rem(along, rows)
    order = jnp.where(down == wanted, 1.0, 0.0).astype(BF16)
    teacher = dot(teacher_ref[...], order, NN)
    target_ref[...] = same + 0.5 * jax.nn.sigmoid(teacher)


def forward(all_ref, w_in_ref, w_out_ref, part_ref):
    blocks, rows, width = part_ref.shape
    pre_act = dot(all_ref[...].reshape(blocks * rows, width), w_in_ref[...], NT)
    value, _ = gelu_both(pre_act)
    part = dot(value.astype(BF16), w_out_ref[...], NN).astype(BF16)
    part = part.reshape(blocks, rows, width)
    for x in range(4):
        for z in range(4):
            part_ref[z * 4 + x] = part[x * 4 + z]


def middle(part_ref, hidden_ref, gain_ref, image_ref, target_ref, out_ref, grad_ref):
    blocks, rows, width = part_ref.shape
    total = part_ref[0].astype(F32)
    for k in range(1, blocks):
        total = total + part_ref[k].astype(F32)
    residual = hidden_ref[...].astype(F32) + total
    gain = gain_ref[...].reshape(1, width)
    normed, inverse = norm_parts(residual)
    final = normed * gain
    length = jnp.sqrt(jnp.sum(final * final, axis=-1, keepdims=True) + epsilon)
    unit = final / length
    images = image_ref[:, :, :, :width].reshape(blocks * rows, width)
    logits = dot(unit.astype(BF16), images, NT) * logit_scale + logit_bias
    pair_grad = (jax.nn.sigmoid(logits) - target_ref[...]).astype(BF16)
    text_grad = logit_scale * dot(pair_grad, images, NN)
    radial = jnp.sum(unit * text_grad, axis=-1, keepdims=True)
    grad_final = (text_grad - unit * radial) / length
    grad = norm_backward(grad_final * gain, normed, inverse)
    grad_ref[...] = grad
    out_ref[...] = grad.astype(BF16)


def backward(all_ref, w_in_ref, rows_ref, w_out_ref, grad_ref, act_ref):
    sides, _, rows, width = rows_ref.shape
    group = sides * sides * rows
    pre_act = dot(all_ref[...].reshape(group, width), w_in_ref[...], NT)
    value, slope = gelu_both(pre_act)
    act_ref[...] = value.astype(BF16)
    grad_act = dot(rows_ref[...].reshape(group, width), w_out_ref[...], NT)
    grad_ref[...] = (grad_act * slope).astype(BF16)


def input_grad(grad_ref, w_in_ref, k0, k1, k2, k3, held):
    at = lax.axis_index("x")
    held[...] = dot(grad_ref[...], w_in_ref[...], NN).astype(BF16).reshape(held.shape)
    for k, out in enumerate((k0, k1, k2, k3)):
        x = lax.rem(at + k, 4)
        for z in range(4):
            out[z] = held[x * 4 + z]


def packed(a_ref, b_ref, out_ref, units, step, width):
    a = a_ref[...]
    full = dot(a, b_ref[...].reshape(a.shape[0], width), TN).astype(out_ref.dtype)
    for c in range(width // LANES):
        out_ref[pl.ds(c * step, units), :] = full[:, c * LANES : (c + 1) * LANES]


def weight_grad(first, step, act_ref, grads_ref, pre_ref, rows_ref, out_ref):
    units = act_ref.shape[1]
    width = grads_ref.shape[-1]
    core = lax.axis_index("co")
    blocks = width // LANES
    for c in range(blocks):
        start = c * step + units // 8 * 8
        stop = (c + 1) * step if c + 1 < blocks else out_ref.shape[0]
        out_ref[start:stop, :] = jnp.zeros((stop - start, LANES), out_ref.dtype)

    @pl.when(core == first)
    def _():
        packed(act_ref, grads_ref, out_ref, units, step, width)

    @pl.when(core != first)
    def _():
        packed(pre_ref, rows_ref, out_ref, units, step, width)


def join(kept_ref, got_ref, out_ref):
    ring, chunk, lanes = out_ref.shape
    total = kept_ref[...] + got_ref[...].astype(F32)
    out_ref[...] = total.astype(BF16).reshape(ring, chunk, lanes)


def ring_sum(slices_ref, out_ref):
    total = slices_ref[0].astype(F32)
    for k in range(1, slices_ref.shape[0]):
        total = total + slices_ref[k].astype(F32)
    sent = total.astype(BF16)
    for k in range(out_ref.shape[0]):
        out_ref[k] = sent


def unpack(step, mine_ref, other_ref, w_out_ref, w_in_ref):
    units, width = w_out_ref.shape
    core = lax.axis_index("co")

    def spread(src, dst):
        for c in range(width // LANES):
            dst[:, c * LANES : (c + 1) * LANES] = src[pl.ds(c * step, units), :].astype(F32)

    @pl.when(core == 0)
    def _():
        spread(mine_ref, w_out_ref)
        spread(other_ref, w_in_ref)

    @pl.when(core != 0)
    def _():
        spread(other_ref, w_out_ref)
        spread(mine_ref, w_in_ref)


def column_sum(k0, k1, k2, k3, keep_ref, sent_ref, held):
    half = lax.axis_index("zh") // 2
    total = k0[...].astype(F32) + k1[...].astype(F32)
    held[...] = total + k2[...].astype(F32) + k3[...].astype(F32)
    for k in range(2):
        keep_ref[k] = held[half * 2 + k]
        sent_ref[k] = held[(1 - half) * 2 + k].astype(BF16)


def pair_sum(kept_ref, got_ref, keep_ref, sent_ref):
    side = lax.rem(lax.axis_index("zh"), 2)
    keep_ref[...] = kept_ref[side] + got_ref[side].astype(F32)
    sent_ref[...] = (kept_ref[1 - side] + got_ref[1 - side].astype(F32)).astype(BF16)


def last(keep_ref, got_ref, hidden_ref, gain_ref, grad_ref, out_ref):
    total = keep_ref[...] + got_ref[...].astype(F32)
    normed, inverse = norm_parts(hidden_ref[...].astype(F32))
    out_ref[...] = grad_ref[...] + norm_backward(total * gain_ref[...].reshape(1, -1), normed, inverse)


def swap(value, axis, by):
    length = lax.axis_size(axis)
    return lax.ppermute(value, axis, [(i, i ^ by) for i in range(length)])


def shift(value, axis, by):
    length = lax.axis_size(axis)
    return lax.ppermute(value, axis, [(i, (i + by) % length) for i in range(length)])


def per_device(
    hidden_in, gain_mlp, gain_final, w_in, w_out, image_embeds, pair_ids, teacher_logits
):
    rows, width = hidden_in.shape
    units = w_in.shape[1]
    blocks = lax.axis_size(BLK)
    ring = lax.axis_size(RING)
    group = rows * blocks
    ids = pair_ids.reshape(1, rows)
    w_in_rows = w_in.T
    teacher = teacher_logits[0].T
    spread = shape((blocks, rows, width), BF16)
    matmul = 2 * group * units * width

    (own_rows,) = call(
        prepare,
        [shape((rows, 2 * width + LANES), BF16)],
        hidden_in,
        gain_mlp,
        image_embeds,
        ids,
        far_in=(0, 1, 2, 3),
        scratch=[
            pltpu.VMEM(hidden_in.shape, BF16),
            pltpu.VMEM(gain_mlp.shape, F32),
            pltpu.VMEM(image_embeds.shape, BF16),
            pltpu.VMEM(ids.shape, ids.dtype),
            pltpu.SemaphoreType.DMA((4,)),
        ],
        grant=WHOLE_GRANT,
    )
    both = lax.all_gather(own_rows, "zh")
    rows_column, column = call(
        split, [shape((4, rows, width), BF16), shape((4, rows, width + LANES), BF16)], both
    )
    group_input = lax.all_gather(rows_column, "x")
    (part,) = call(forward, [spread], group_input, w_in_rows, w_out, flops=2 * matmul)
    part, column = lax.optimization_barrier((part, column))
    images = lax.all_gather(column, "x")
    (target,) = call(targets, [shape((rows, group), F32)], images, teacher, ids)
    parts = lax.all_to_all(part, BLK, 0, 0)
    own_grads, grad_residual = call(
        middle,
        [shape((rows, width), BF16), shape((rows, width), F32)],
        parts,
        hidden_in,
        gain_final,
        images,
        target,
    )
    group_grads = lax.all_gather(lax.all_gather(own_grads, "zh"), "x")
    grad_pre, act = call(
        backward,
        [shape((group, units), BF16)] * 2,
        group_input,
        w_in_rows,
        group_grads,
        w_out,
        flops=2 * matmul,
    )

    step = -(-units // 16) * 16
    chunk = -(-(step * (width // LANES)) // (8 * ring)) * 8
    tall = chunk * ring

    def grads(first, dtype):
        return call(
            lambda *refs: weight_grad(first, step, *refs),
            [shape((tall, LANES), dtype)],
            act,
            group_grads,
            grad_pre,
            group_input,
            flops=matmul,
        )[0]

    give = grads(1, BF16)
    got = shift(give, "co", 1)
    keep = grads(0, F32)
    (mine,) = call(join, [shape((ring, chunk, LANES), BF16)], keep, got)
    slices = lax.all_to_all(mine, RING, 0, 0)

    quarter = shape((4, rows, width), BF16)
    k0, s1, s2, s3 = call(
        input_grad,
        [quarter] * 4,
        grad_pre,
        w_in_rows,
        flops=matmul,
        scratch=[pltpu.VMEM((blocks, rows, width), BF16)],
    )
    arrived = []
    for k, sent in ((1, s1), (2, s2), (3, s3)):
        arrived.append(shift(sent, "x", k))
    kept, sent = call(
        column_sum,
        [shape((2, rows, width), F32), shape((2, rows, width), BF16)],
        k0,
        *arrived,
        scratch=[pltpu.VMEM((4, rows, width), F32)],
    )
    got = swap(sent, "zh", 2)
    own, sent = call(pair_sum, [shape((rows, width), F32), shape((rows, width), BF16)], kept, got)
    got = swap(sent, "zh", 1)
    (grad_hidden,) = call(
        last, [shape((rows, width), F32)], own, got, hidden_in, gain_mlp, grad_residual
    )

    (copies,) = call(ring_sum, [shape((ring, chunk, LANES), BF16)], slices)
    whole = lax.all_to_all(copies, RING, 0, 0).reshape(tall, LANES)
    other = shift(whole, "co", 1)
    grad_w_out, grad_w_in = call(
        lambda *refs: unpack(step, *refs), [shape((units, width), F32)] * 2, whole, other
    )
    return (grad_hidden, grad_w_in.T, grad_w_out)


def solution(mesh):
    fine = Mesh(mesh.devices.reshape(2, 8, 2, 4, 4), ("zl", "y", "co", "zh", "x"))
    every = DP + BLK
    in_specs = (
        P(every, None),
        P(),
        P(),
        P(None, BLK),
        P(BLK, None),
        P(every, None),
        P(every),
        P(DP, None, BLK),
    )
    out_specs = (P(every, None), P(None, BLK), P(BLK, None))
    return jax.shard_map(
        per_device, mesh=fine, in_specs=in_specs, out_specs=out_specs, check_vma=False
    )
```

```python
import jax
import jax.numpy as jnp
from jax import lax
from jax.experimental import pallas as pl
from jax.experimental.pallas import tpu as pltpu
from jax.sharding import Mesh
from jax.sharding import PartitionSpec as P


epsilon = 1e-06
logit_scale = 10.0
logit_bias = -2.0
gelu_coeff = 0.7978845608028654

DP = ("zl", "y", "co")
BLK = ("zh", "x")
ARRIVAL = ("x", "zh")
RING = ("zl", "y")
LANES = 128
VMEM_GRANT = 8 * 2**20
WHOLE_GRANT = 60 * 2**20
F32 = jnp.float32
BF16 = jnp.bfloat16

NT = (((1,), (1,)), ((), ()))
TN = (((0,), (0,)), ((), ()))
NN = (((1,), (0,)), ((), ()))


def shape(dims, dtype):
    return jax.ShapeDtypeStruct(dims, dtype)


def call(body, outs, *args, far_in=(), scratch=(), flops=0, grant=VMEM_GRANT):
    size = sum(a.size * a.dtype.itemsize for a in args)
    size += sum(o.size * o.dtype.itemsize for o in outs)
    near = pl.BlockSpec(memory_space=pltpu.VMEM)
    far = pl.BlockSpec(memory_space=pl.ANY)
    return pl.pallas_call(
        body,
        out_shape=tuple(outs),
        in_specs=[far if k in far_in else near for k in range(len(args))],
        out_specs=tuple([near] * len(outs)),
        scratch_shapes=list(scratch),
        compiler_params=pltpu.CompilerParams(vmem_limit_bytes=grant),
        cost_estimate=pl.CostEstimate(flops=flops, bytes_accessed=size, transcendentals=0),
    )(*args)


def dot(a, b, dims):
    return lax.dot_general(a, b, dims, preferred_element_type=F32)


def norm_parts(values):
    row_mean = jnp.mean(values, axis=-1, keepdims=True)
    centred = values - row_mean
    variance = jnp.mean(centred * centred, axis=-1, keepdims=True)
    inverse = lax.rsqrt(variance + epsilon)
    return centred * inverse, inverse


def norm_backward(grad_normed, normed, inverse):
    mean_grad = jnp.mean(grad_normed, axis=-1, keepdims=True)
    mean_cross = jnp.mean(grad_normed * normed, axis=-1, keepdims=True)
    return inverse * (grad_normed - mean_grad - normed * mean_cross)


def gelu_both(pre_act):
    inner_arg = gelu_coeff * (pre_act + 0.044715 * pre_act * pre_act * pre_act)
    tangent = jnp.tanh(inner_arg)
    gelu_value = 0.5 * pre_act * (1.0 + tangent)
    gelu_slope = 0.5 * (1.0 + tangent) + 0.5 * pre_act * (1.0 - tangent * tangent) * gelu_coeff * (
        1.0 + 3.0 * 0.044715 * pre_act * pre_act
    )
    return gelu_value, gelu_slope


def column_of(row_ref):
    count = row_ref.shape[1]
    spread = jnp.broadcast_to(row_ref[...], (count, count))
    down = lax.broadcasted_iota(jnp.int32, (count, count), 0)
    along = lax.broadcasted_iota(jnp.int32, (count, count), 1)
    return jnp.sum(jnp.where(down == along, spread, 0), axis=1, keepdims=True)


def prepare(
    hidden_hbm, gain_hbm, image_hbm, id_hbm, out_ref, hidden_ref, gain_ref, image_ref, id_ref, sems
):
    width = hidden_ref.shape[1]
    arrays = ((hidden_hbm, hidden_ref), (gain_hbm, gain_ref), (image_hbm, image_ref), (id_hbm, id_ref))
    moves = [pltpu.make_async_copy(src, dst, sems.at[k]) for k, (src, dst) in enumerate(arrays)]
    for move in moves:
        move.start()
    for move in moves:
        move.wait()
    normed, _ = norm_parts(hidden_ref[...].astype(F32))
    out_ref[:, :width] = (normed * gain_ref[...].reshape(1, width)).astype(BF16)
    image = image_ref[...].astype(F32)
    scale = lax.rsqrt(jnp.sum(image * image, axis=-1, keepdims=True) + epsilon)
    out_ref[:, width : 2 * width] = (image * scale).astype(BF16)
    ids = column_of(id_ref)
    lane = lax.broadcasted_iota(jnp.int32, (image.shape[0], LANES), 1)
    low = jnp.where(lane == 0, ids & 127, 0)
    high = jnp.where(lane == 1, ids >> 7, 0)
    out_ref[:, 2 * width :] = (low + high).astype(F32).astype(BF16)


def split(both_ref, rows_ref, image_ref):
    width = rows_ref.shape[2]
    rows_ref[...] = both_ref[:, :, :width]
    image_ref[...] = both_ref[:, :, width:]


def targets(image_ref, teacher_ref, id_ref, target_ref):
    sides, _, rows, deep = image_ref.shape
    group = sides * sides * rows
    marks = image_ref[:, :, :, deep - LANES :].reshape(group, LANES)
    row = lax.broadcasted_iota(jnp.int32, (8, LANES), 0)
    lane = lax.broadcasted_iota(jnp.int32, (8, LANES), 1)
    pick = jnp.where(row == lane, 1.0, 0.0).astype(BF16)
    ids = dot(pick, marks, NT)
    image_id = ids[0:1] + 128.0 * ids[1:2]
    text_id = column_of(id_ref).astype(F32)
    same = jnp.where(text_id == image_id, 0.5, 0.0)
    down = lax.broadcasted_iota(jnp.int32, (group, group), 0)
    along = lax.broadcasted_iota(jnp.int32, (1, group), 1)
    block = along // rows
    wanted = (lax.rem(block, sides) * sides + block // sides) * rows + lax.rem(along, rows)
    order = jnp.where(down == wanted, 1.0, 0.0).astype(BF16)
    teacher = dot(teacher_ref[...], order, NN)
    target_ref[...] = same + 0.5 * jax.nn.sigmoid(teacher)


def forward(all_ref, w_in_ref, w_out_ref, part_ref):
    blocks, rows, width = part_ref.shape
    pre_act = dot(all_ref[...].reshape(blocks * rows, width), w_in_ref[...], NT)
    value, _ = gelu_both(pre_act)
    part = dot(value.astype(BF16), w_out_ref[...], NN).astype(BF16)
    part_ref[...] = part.reshape(blocks, rows, width)


def middle(part_ref, hidden_ref, gain_ref, image_ref, target_ref, out_ref, grad_ref):
    blocks, rows, width = part_ref.shape
    total = part_ref[0].astype(F32)
    for k in range(1, blocks):
        total = total + part_ref[k].astype(F32)
    residual = hidden_ref[...].astype(F32) + total
    gain = gain_ref[...].reshape(1, width)
    normed, inverse = norm_parts(residual)
    final = normed * gain
    length = jnp.sqrt(jnp.sum(final * final, axis=-1, keepdims=True) + epsilon)
    unit = final / length
    images = image_ref[:, :, :, :width].reshape(blocks * rows, width)
    logits = dot(unit.astype(BF16), images, NT) * logit_scale + logit_bias
    pair_grad = (jax.nn.sigmoid(logits) - target_ref[...]).astype(BF16)
    text_grad = logit_scale * dot(pair_grad, images, NN)
    radial = jnp.sum(unit * text_grad, axis=-1, keepdims=True)
    grad_final = (text_grad - unit * radial) / length
    grad = norm_backward(grad_final * gain, normed, inverse)
    grad_ref[...] = grad
    sent = grad.astype(BF16)
    for k in range(blocks):
        out_ref[k] = sent


def backward(all_ref, w_in_ref, rows_ref, w_out_ref, grad_ref, act_ref):
    blocks, rows, width = rows_ref.shape
    group = blocks * rows
    pre_act = dot(all_ref[...].reshape(group, width), w_in_ref[...], NT)
    value, slope = gelu_both(pre_act)
    act_ref[...] = value.astype(BF16)
    grad_act = dot(rows_ref[...].reshape(group, width), w_out_ref[...], NT)
    grad_ref[...] = (grad_act * slope).astype(BF16)


def input_grad(grad_ref, w_in_ref, k0, k1, k2, k3, held):
    at = lax.axis_index("x")
    held[...] = dot(grad_ref[...], w_in_ref[...], NN).astype(BF16).reshape(held.shape)
    for k, out in enumerate((k0, k1, k2, k3)):
        x = lax.rem(at + k, 4)
        for z in range(4):
            out[z] = held[x * 4 + z]


def packed(a_ref, b_ref, out_ref):
    a = a_ref[...]
    units = a.shape[1]
    width = b_ref.shape[-1]
    blocks = width // LANES
    even = units // 8 * 8
    odd = units - even
    full = dot(a, b_ref[...].reshape(a.shape[0], width), TN).astype(out_ref.dtype)
    for c in range(blocks):
        tile = full[:, c * LANES : (c + 1) * LANES]
        out_ref[c * even : (c + 1) * even, :] = tile[:even]
        if odd:
            out_ref[blocks * even + c * odd : blocks * even + (c + 1) * odd, :] = tile[even:]


def weight_grad(first, act_ref, grads_ref, pre_ref, rows_ref, out_ref):
    units = act_ref.shape[1]
    width = grads_ref.shape[-1]
    core = lax.axis_index("co")
    used = units * (width // LANES) // 8 * 8
    tall = out_ref.shape[0]
    if used < tall:
        out_ref[used:tall, :] = jnp.zeros((tall - used, LANES), out_ref.dtype)

    @pl.when(core == first)
    def _():
        packed(act_ref, grads_ref, out_ref)

    @pl.when(core != first)
    def _():
        packed(pre_ref, rows_ref, out_ref)


def join(kept_ref, got_ref, out_ref):
    ring, chunk, lanes = out_ref.shape
    total = kept_ref[...] + got_ref[...].astype(F32)
    out_ref[...] = total.astype(BF16).reshape(ring, chunk, lanes)


def ring_sum(slices_ref, out_ref):
    total = slices_ref[0].astype(F32)
    for k in range(1, slices_ref.shape[0]):
        total = total + slices_ref[k].astype(F32)
    sent = total.astype(BF16)
    for k in range(out_ref.shape[0]):
        out_ref[k] = sent


def unpack(mine_ref, other_ref, w_out_ref, w_in_ref):
    units, width = w_out_ref.shape
    core = lax.axis_index("co")
    blocks = width // LANES
    even = units // 8 * 8
    odd = units - even

    def spread(src, dst):
        for c in range(blocks):
            lanes = slice(c * LANES, (c + 1) * LANES)
            dst[:even, lanes] = src[c * even : (c + 1) * even, :].astype(F32)
            if odd:
                at = blocks * even + c * odd
                dst[even:, lanes] = src[at : at + odd, :].astype(F32)

    @pl.when(core == 0)
    def _():
        spread(mine_ref, w_out_ref)
        spread(other_ref, w_in_ref)

    @pl.when(core != 0)
    def _():
        spread(other_ref, w_out_ref)
        spread(mine_ref, w_in_ref)


def column_sum(k0, k1, k2, k3, keep_ref, s1, s2, s3, held):
    at = lax.axis_index("zh")
    total = k0[...].astype(F32) + k1[...].astype(F32)
    held[...] = total + k2[...].astype(F32) + k3[...].astype(F32)
    keep_ref[...] = held[at]
    for k, out in enumerate((s1, s2, s3)):
        out[...] = held[lax.rem(at + k + 1, 4)].astype(BF16)


def last(keep_ref, g1, g2, g3, hidden_ref, gain_ref, grad_ref, out_ref):
    total = keep_ref[...] + g1[...].astype(F32) + g2[...].astype(F32) + g3[...].astype(F32)
    normed, inverse = norm_parts(hidden_ref[...].astype(F32))
    out_ref[...] = grad_ref[...] + norm_backward(total * gain_ref[...].reshape(1, -1), normed, inverse)


def shift(value, axis, by):
    length = lax.axis_size(axis)
    return lax.ppermute(value, axis, [(i, (i + by) % length) for i in range(length)])


def per_device(
    hidden_in, gain_mlp, gain_final, w_in, w_out, image_embeds, pair_ids, teacher_logits
):
    rows, width = hidden_in.shape
    units = w_in.shape[1]
    blocks = lax.axis_size(BLK)
    ring = lax.axis_size(RING)
    group = rows * blocks
    ids = pair_ids.reshape(1, rows)
    w_in_rows = w_in.T
    teacher = teacher_logits[0].T
    spread = shape((blocks, rows, width), BF16)
    matmul = 2 * group * units * width

    (own_rows,) = call(
        prepare,
        [shape((rows, 2 * width + LANES), BF16)],
        hidden_in,
        gain_mlp,
        image_embeds,
        ids,
        far_in=(0, 1, 2, 3),
        scratch=[
            pltpu.VMEM(hidden_in.shape, BF16),
            pltpu.VMEM(gain_mlp.shape, F32),
            pltpu.VMEM(image_embeds.shape, BF16),
            pltpu.VMEM(ids.shape, ids.dtype),
            pltpu.SemaphoreType.DMA((4,)),
        ],
        grant=WHOLE_GRANT,
    )
    both = lax.all_gather(own_rows, "zh")
    rows_column, column = call(
        split, [shape((4, rows, width), BF16), shape((4, rows, width + LANES), BF16)], both
    )
    group_input = lax.all_gather(rows_column, "x")
    (part,) = call(forward, [spread], group_input, w_in_rows, w_out, flops=2 * matmul)
    part, column = lax.optimization_barrier((part, column))
    images = lax.all_gather(column, "x")
    (target,) = call(targets, [shape((rows, group), F32)], images, teacher, ids)
    parts = lax.all_to_all(part, ARRIVAL, 0, 0)
    copies, grad_residual = call(
        middle, [spread, shape((rows, width), F32)], parts, hidden_in, gain_final, images, target
    )
    group_grads = lax.all_to_all(copies, ARRIVAL, 0, 0)
    grad_pre, act = call(
        backward,
        [shape((group, units), BF16)] * 2,
        group_input,
        w_in_rows,
        group_grads,
        w_out,
        flops=2 * matmul,
    )

    chunk = -(-(units * (width // LANES)) // (8 * ring)) * 8
    tall = chunk * ring

    def grads(first, dtype):
        return call(
            lambda *refs: weight_grad(first, *refs),
            [shape((tall, LANES), dtype)],
            act,
            group_grads,
            grad_pre,
            group_input,
            flops=matmul,
        )[0]

    give = grads(1, BF16)
    got = shift(give, "co", 1)
    keep = grads(0, F32)
    (mine,) = call(join, [shape((ring, chunk, LANES), BF16)], keep, got)
    slices = lax.all_to_all(mine, RING, 0, 0)

    quarter = shape((4, rows, width), BF16)
    k0, s1, s2, s3 = call(
        input_grad,
        [quarter] * 4,
        grad_pre,
        w_in_rows,
        flops=matmul,
        scratch=[pltpu.VMEM((blocks, rows, width), BF16)],
    )
    arrived = []
    for k, sent in ((1, s1), (2, s2), (3, s3)):
        arrived.append(shift(sent, "x", k))
    own, s1, s2, s3 = call(
        column_sum,
        [shape((rows, width), F32)] + [shape((rows, width), BF16)] * 3,
        k0,
        *arrived,
        scratch=[pltpu.VMEM((4, rows, width), F32)],
    )
    arrived = []
    for k, sent in ((1, s1), (2, s2), (3, s3)):
        arrived.append(shift(sent, "zh", k))
    (grad_hidden,) = call(
        last, [shape((rows, width), F32)], own, *arrived, hidden_in, gain_mlp, grad_residual
    )

    (copies,) = call(ring_sum, [shape((ring, chunk, LANES), BF16)], slices)
    whole = lax.all_to_all(copies, RING, 0, 0).reshape(tall, LANES)
    other = shift(whole, "co", 1)
    grad_w_out, grad_w_in = call(unpack, [shape((units, width), F32)] * 2, whole, other)
    return (grad_hidden, grad_w_in.T, grad_w_out)


def solution(mesh):
    fine = Mesh(mesh.devices.reshape(2, 8, 2, 4, 4), ("zl", "y", "co", "zh", "x"))
    every = DP + BLK
    in_specs = (
        P(every, None),
        P(),
        P(),
        P(None, BLK),
        P(BLK, None),
        P(every, None),
        P(every),
        P(DP, None, BLK),
    )
    out_specs = (P(every, None), P(None, BLK), P(BLK, None))
    return jax.shard_map(
        per_device, mesh=fine, in_specs=in_specs, out_specs=out_specs, check_vma=False
    )
```

```python
import jax
import jax.numpy as jnp
from jax import lax
from jax.experimental import pallas as pl
from jax.experimental.pallas import tpu as pltpu
from jax.sharding import Mesh
from jax.sharding import PartitionSpec as P


epsilon = 1e-06
logit_scale = 10.0
logit_bias = -2.0
gelu_coeff = 0.7978845608028654

DP = ("zl", "y", "co")
BLK = ("zh", "x")
ARRIVAL = ("x", "zh")
RING = ("zl", "y")
LANES = 128
VMEM_GRANT = 8 * 2**20
WHOLE_GRANT = 60 * 2**20
F32 = jnp.float32
BF16 = jnp.bfloat16

NT = (((1,), (1,)), ((), ()))
TN = (((0,), (0,)), ((), ()))
NN = (((1,), (0,)), ((), ()))


def shape(dims, dtype):
    return jax.ShapeDtypeStruct(dims, dtype)


def call(body, outs, *args, far_in=(), scratch=(), flops=0, grant=VMEM_GRANT):
    size = sum(a.size * a.dtype.itemsize for a in args)
    size += sum(o.size * o.dtype.itemsize for o in outs)
    near = pl.BlockSpec(memory_space=pltpu.VMEM)
    far = pl.BlockSpec(memory_space=pl.ANY)
    return pl.pallas_call(
        body,
        out_shape=tuple(outs),
        in_specs=[far if k in far_in else near for k in range(len(args))],
        out_specs=tuple([near] * len(outs)),
        scratch_shapes=list(scratch),
        compiler_params=pltpu.CompilerParams(vmem_limit_bytes=grant),
        cost_estimate=pl.CostEstimate(flops=flops, bytes_accessed=size, transcendentals=0),
    )(*args)


def dot(a, b, dims):
    return lax.dot_general(a, b, dims, preferred_element_type=F32)


def norm_parts(values):
    row_mean = jnp.mean(values, axis=-1, keepdims=True)
    centred = values - row_mean
    variance = jnp.mean(centred * centred, axis=-1, keepdims=True)
    inverse = lax.rsqrt(variance + epsilon)
    return centred * inverse, inverse


def norm_backward(grad_normed, normed, inverse):
    mean_grad = jnp.mean(grad_normed, axis=-1, keepdims=True)
    mean_cross = jnp.mean(grad_normed * normed, axis=-1, keepdims=True)
    return inverse * (grad_normed - mean_grad - normed * mean_cross)


def gelu_both(pre_act):
    inner_arg = gelu_coeff * (pre_act + 0.044715 * pre_act * pre_act * pre_act)
    tangent = jnp.tanh(inner_arg)
    gelu_value = 0.5 * pre_act * (1.0 + tangent)
    gelu_slope = 0.5 * (1.0 + tangent) + 0.5 * pre_act * (1.0 - tangent * tangent) * gelu_coeff * (
        1.0 + 3.0 * 0.044715 * pre_act * pre_act
    )
    return gelu_value, gelu_slope


def column_of(row_ref):
    count = row_ref.shape[1]
    spread = jnp.broadcast_to(row_ref[...], (count, count))
    down = lax.broadcasted_iota(jnp.int32, (count, count), 0)
    along = lax.broadcasted_iota(jnp.int32, (count, count), 1)
    return jnp.sum(jnp.where(down == along, spread, 0), axis=1, keepdims=True)


def prepare(
    hidden_hbm, gain_hbm, image_hbm, id_hbm, out_ref, hidden_ref, gain_ref, image_ref, id_ref, sems
):
    width = hidden_ref.shape[1]
    arrays = ((hidden_hbm, hidden_ref), (gain_hbm, gain_ref), (image_hbm, image_ref), (id_hbm, id_ref))
    moves = [pltpu.make_async_copy(src, dst, sems.at[k]) for k, (src, dst) in enumerate(arrays)]
    for move in moves:
        move.start()
    for move in moves:
        move.wait()
    normed, _ = norm_parts(hidden_ref[...].astype(F32))
    out_ref[:, :width] = (normed * gain_ref[...].reshape(1, width)).astype(BF16)
    image = image_ref[...].astype(F32)
    scale = lax.rsqrt(jnp.sum(image * image, axis=-1, keepdims=True) + epsilon)
    out_ref[:, width : 2 * width] = (image * scale).astype(BF16)
    ids = column_of(id_ref)
    lane = lax.broadcasted_iota(jnp.int32, (image.shape[0], LANES), 1)
    low = jnp.where(lane == 0, ids & 127, 0)
    high = jnp.where(lane == 1, ids >> 7, 0)
    out_ref[:, 2 * width :] = (low + high).astype(F32).astype(BF16)


def split(both_ref, rows_ref, image_ref):
    width = rows_ref.shape[2]
    rows_ref[...] = both_ref[:, :, :width]
    image_ref[...] = both_ref[:, :, width:]


def targets(image_ref, teacher_ref, id_ref, target_ref):
    sides, _, rows, deep = image_ref.shape
    group = sides * sides * rows
    marks = image_ref[:, :, :, deep - LANES :].reshape(group, LANES)
    row = lax.broadcasted_iota(jnp.int32, (8, LANES), 0)
    lane = lax.broadcasted_iota(jnp.int32, (8, LANES), 1)
    pick = jnp.where(row == lane, 1.0, 0.0).astype(BF16)
    ids = dot(pick, marks, NT)
    image_id = ids[0:1] + 128.0 * ids[1:2]
    text_id = column_of(id_ref).astype(F32)
    same = jnp.where(text_id == image_id, 0.5, 0.0)
    down = lax.broadcasted_iota(jnp.int32, (group, group), 0)
    along = lax.broadcasted_iota(jnp.int32, (1, group), 1)
    block = along // rows
    wanted = (lax.rem(block, sides) * sides + block // sides) * rows + lax.rem(along, rows)
    order = jnp.where(down == wanted, 1.0, 0.0).astype(BF16)
    teacher = dot(teacher_ref[...], order, NN)
    target_ref[...] = same + 0.5 * jax.nn.sigmoid(teacher)


def forward(all_ref, w_in_ref, w_out_ref, part_ref):
    blocks, rows, width = part_ref.shape
    pre_act = dot(all_ref[...].reshape(blocks * rows, width), w_in_ref[...], NT)
    value, _ = gelu_both(pre_act)
    part = dot(value.astype(BF16), w_out_ref[...], NN).astype(BF16)
    part_ref[...] = part.reshape(blocks, rows, width)


def middle(part_ref, hidden_ref, gain_ref, image_ref, target_ref, out_ref, grad_ref):
    blocks, rows, width = part_ref.shape
    total = part_ref[0].astype(F32)
    for k in range(1, blocks):
        total = total + part_ref[k].astype(F32)
    residual = hidden_ref[...].astype(F32) + total
    gain = gain_ref[...].reshape(1, width)
    normed, inverse = norm_parts(residual)
    final = normed * gain
    length = jnp.sqrt(jnp.sum(final * final, axis=-1, keepdims=True) + epsilon)
    unit = final / length
    images = image_ref[:, :, :, :width].reshape(blocks * rows, width)
    logits = dot(unit.astype(BF16), images, NT) * logit_scale + logit_bias
    pair_grad = (jax.nn.sigmoid(logits) - target_ref[...]).astype(BF16)
    text_grad = logit_scale * dot(pair_grad, images, NN)
    radial = jnp.sum(unit * text_grad, axis=-1, keepdims=True)
    grad_final = (text_grad - unit * radial) / length
    grad = norm_backward(grad_final * gain, normed, inverse)
    grad_ref[...] = grad
    sent = grad.astype(BF16)
    for k in range(blocks):
        out_ref[k] = sent


def backward(all_ref, w_in_ref, rows_ref, w_out_ref, grad_ref, act_ref):
    blocks, rows, width = rows_ref.shape
    group = blocks * rows
    pre_act = dot(all_ref[...].reshape(group, width), w_in_ref[...], NT)
    value, slope = gelu_both(pre_act)
    act_ref[...] = value.astype(BF16)
    grad_act = dot(rows_ref[...].reshape(group, width), w_out_ref[...], NT)
    grad_ref[...] = (grad_act * slope).astype(BF16)


def input_grad(grad_ref, w_in_ref, k0, k1, k2, k3, held):
    at = lax.axis_index("x")
    held[...] = dot(grad_ref[...], w_in_ref[...], NN).astype(BF16).reshape(held.shape)
    for k, out in enumerate((k0, k1, k2, k3)):
        x = lax.rem(at + k, 4)
        for z in range(4):
            out[z] = held[x * 4 + z]


def packed(a_ref, b_ref, out_ref):
    a = a_ref[...]
    units = a.shape[1]
    width = b_ref.shape[-1]
    blocks = width // LANES
    even = units // 8 * 8
    odd = units - even
    full = dot(a, b_ref[...].reshape(a.shape[0], width), TN).astype(out_ref.dtype)
    for c in range(blocks):
        tile = full[:, c * LANES : (c + 1) * LANES]
        out_ref[c * even : (c + 1) * even, :] = tile[:even]
        if odd:
            out_ref[blocks * even + c * odd : blocks * even + (c + 1) * odd, :] = tile[even:]


def weight_grad(first, act_ref, grads_ref, pre_ref, rows_ref, out_ref):
    units = act_ref.shape[1]
    width = grads_ref.shape[-1]
    core = lax.axis_index("co")
    used = units * (width // LANES) // 8 * 8
    tall = out_ref.shape[0]
    if used < tall:
        out_ref[used:tall, :] = jnp.zeros((tall - used, LANES), out_ref.dtype)

    @pl.when(core == first)
    def _():
        packed(act_ref, grads_ref, out_ref)

    @pl.when(core != first)
    def _():
        packed(pre_ref, rows_ref, out_ref)


def join(kept_ref, got_ref, out_ref):
    ring, chunk, lanes = out_ref.shape
    total = kept_ref[...] + got_ref[...].astype(F32)
    out_ref[...] = total.astype(BF16).reshape(ring, chunk, lanes)


def ring_sum(slices_ref, out_ref):
    total = slices_ref[0].astype(F32)
    for k in range(1, slices_ref.shape[0]):
        total = total + slices_ref[k].astype(F32)
    sent = total.astype(BF16)
    for k in range(out_ref.shape[0]):
        out_ref[k] = sent


def unpack(owner, src_ref, *refs):
    w_out_hbm, w_in_hbm, full_ref, sem = refs[-4:]
    units, width = full_ref.shape
    core = lax.axis_index("co")
    blocks = width // LANES
    even = units // 8 * 8
    odd = units - even
    for c in range(blocks):
        lanes = slice(c * LANES, (c + 1) * LANES)
        full_ref[:even, lanes] = src_ref[c * even : (c + 1) * even, :].astype(F32)
        if odd:
            at = blocks * even + c * odd
            full_ref[even:, lanes] = src_ref[at : at + odd, :].astype(F32)

    @pl.when(core == owner)
    def _():
        move = pltpu.make_async_copy(full_ref, w_out_hbm, sem)
        move.start()
        move.wait()

    @pl.when(core != owner)
    def _():
        move = pltpu.make_async_copy(full_ref, w_in_hbm, sem)
        move.start()
        move.wait()


def column_sum(k0, k1, k2, k3, keep_ref, s1, s2, s3, held):
    at = lax.axis_index("zh")
    total = k0[...].astype(F32) + k1[...].astype(F32)
    held[...] = total + k2[...].astype(F32) + k3[...].astype(F32)
    keep_ref[...] = held[at]
    for k, out in enumerate((s1, s2, s3)):
        out[...] = held[lax.rem(at + k + 1, 4)].astype(BF16)


def last(keep_ref, g1, g2, g3, hidden_ref, gain_ref, grad_ref, out_ref):
    total = keep_ref[...] + g1[...].astype(F32) + g2[...].astype(F32) + g3[...].astype(F32)
    normed, inverse = norm_parts(hidden_ref[...].astype(F32))
    out_ref[...] = grad_ref[...] + norm_backward(total * gain_ref[...].reshape(1, -1), normed, inverse)


def shift(value, axis, by):
    length = lax.axis_size(axis)
    return lax.ppermute(value, axis, [(i, (i + by) % length) for i in range(length)])


def unpack_call(owner, src, whole, units, width):
    far = pl.BlockSpec(memory_space=pl.ANY)
    near = pl.BlockSpec(memory_space=pltpu.VMEM)
    return pl.pallas_call(
        lambda *refs: unpack(owner, *refs),
        out_shape=(shape((units, width), F32),) * 2,
        in_specs=[near] + [far] * len(whole),
        out_specs=(far, far),
        scratch_shapes=[pltpu.VMEM((units, width), F32), pltpu.SemaphoreType.DMA(())],
        input_output_aliases={k + 1: k for k in range(len(whole))},
        compiler_params=pltpu.CompilerParams(vmem_limit_bytes=VMEM_GRANT),
        cost_estimate=pl.CostEstimate(
            flops=0, bytes_accessed=6 * units * width, transcendentals=0
        ),
    )(src, *whole)


def per_device(
    hidden_in, gain_mlp, gain_final, w_in, w_out, image_embeds, pair_ids, teacher_logits
):
    rows, width = hidden_in.shape
    units = w_in.shape[1]
    blocks = lax.axis_size(BLK)
    ring = lax.axis_size(RING)
    group = rows * blocks
    ids = pair_ids.reshape(1, rows)
    w_in_rows = w_in.T
    teacher = teacher_logits[0].T
    spread = shape((blocks, rows, width), BF16)
    matmul = 2 * group * units * width

    (own_rows,) = call(
        prepare,
        [shape((rows, 2 * width + LANES), BF16)],
        hidden_in,
        gain_mlp,
        image_embeds,
        ids,
        far_in=(0, 1, 2, 3),
        scratch=[
            pltpu.VMEM(hidden_in.shape, BF16),
            pltpu.VMEM(gain_mlp.shape, F32),
            pltpu.VMEM(image_embeds.shape, BF16),
            pltpu.VMEM(ids.shape, ids.dtype),
            pltpu.SemaphoreType.DMA((4,)),
        ],
        grant=WHOLE_GRANT,
    )
    both = lax.all_gather(own_rows, "zh")
    rows_column, column = call(
        split, [shape((4, rows, width), BF16), shape((4, rows, width + LANES), BF16)], both
    )
    group_input = lax.all_gather(rows_column, "x")
    (part,) = call(forward, [spread], group_input, w_in_rows, w_out, flops=2 * matmul)
    part, column = lax.optimization_barrier((part, column))
    images = lax.all_gather(column, "x")
    (target,) = call(targets, [shape((rows, group), F32)], images, teacher, ids)
    parts = lax.all_to_all(part, ARRIVAL, 0, 0)
    copies, grad_residual = call(
        middle, [spread, shape((rows, width), F32)], parts, hidden_in, gain_final, images, target
    )
    group_grads = lax.all_to_all(copies, ARRIVAL, 0, 0)
    grad_pre, act = call(
        backward,
        [shape((group, units), BF16)] * 2,
        group_input,
        w_in_rows,
        group_grads,
        w_out,
        flops=2 * matmul,
    )

    chunk = -(-(units * (width // LANES)) // (8 * ring)) * 8
    tall = chunk * ring

    def grads(first, dtype):
        return call(
            lambda *refs: weight_grad(first, *refs),
            [shape((tall, LANES), dtype)],
            act,
            group_grads,
            grad_pre,
            group_input,
            flops=matmul,
        )[0]

    give = grads(1, BF16)
    got = shift(give, "co", 1)
    keep = grads(0, F32)
    (mine,) = call(join, [shape((ring, chunk, LANES), BF16)], keep, got)
    slices = lax.all_to_all(mine, RING, 0, 0)

    quarter = shape((4, rows, width), BF16)
    k0, s1, s2, s3 = call(
        input_grad,
        [quarter] * 4,
        grad_pre,
        w_in_rows,
        flops=matmul,
        scratch=[pltpu.VMEM((blocks, rows, width), BF16)],
    )
    arrived = []
    for k, sent in ((1, s1), (2, s2), (3, s3)):
        arrived.append(shift(sent, "x", k))
    own, s1, s2, s3 = call(
        column_sum,
        [shape((rows, width), F32)] + [shape((rows, width), BF16)] * 3,
        k0,
        *arrived,
        scratch=[pltpu.VMEM((4, rows, width), F32)],
    )
    arrived = []
    for k, sent in ((1, s1), (2, s2), (3, s3)):
        arrived.append(shift(sent, "zh", k))
    (grad_hidden,) = call(
        last, [shape((rows, width), F32)], own, *arrived, hidden_in, gain_mlp, grad_residual
    )

    (copies,) = call(ring_sum, [shape((ring, chunk, LANES), BF16)], slices)
    whole = lax.all_to_all(copies, RING, 0, 0).reshape(tall, LANES)
    other = shift(whole, "co", 1)
    grad_w_out, grad_w_in = unpack_call(0, whole, (), units, width)
    grad_w_out, grad_w_in = unpack_call(1, other, (grad_w_out, grad_w_in), units, width)
    return (grad_hidden, grad_w_in.T, grad_w_out)


def solution(mesh):
    fine = Mesh(mesh.devices.reshape(2, 8, 2, 4, 4), ("zl", "y", "co", "zh", "x"))
    every = DP + BLK
    in_specs = (
        P(every, None),
        P(),
        P(),
        P(None, BLK),
        P(BLK, None),
        P(every, None),
        P(every),
        P(DP, None, BLK),
    )
    out_specs = (P(every, None), P(None, BLK), P(BLK, None))
    return jax.shard_map(
        per_device, mesh=fine, in_specs=in_specs, out_specs=out_specs, check_vma=False
    )
```

```python
import jax
import jax.numpy as jnp
from jax import lax
from jax.experimental import pallas as pl
from jax.experimental.pallas import tpu as pltpu
from jax.sharding import Mesh
from jax.sharding import PartitionSpec as P


epsilon = 1e-06
logit_scale = 10.0
logit_bias = -2.0
gelu_coeff = 0.7978845608028654

DP = ("zl", "y", "co")
BLK = ("zh", "x")
ARRIVAL = ("x", "zh")
RING = ("zl", "y")
LANES = 128
VMEM_GRANT = 8 * 2**20
WHOLE_GRANT = 60 * 2**20
F32 = jnp.float32
BF16 = jnp.bfloat16

NT = (((1,), (1,)), ((), ()))
TN = (((0,), (0,)), ((), ()))
NN = (((1,), (0,)), ((), ()))


def shape(dims, dtype):
    return jax.ShapeDtypeStruct(dims, dtype)


def call(body, outs, *args, far_in=(), scratch=(), flops=0, grant=VMEM_GRANT):
    size = sum(a.size * a.dtype.itemsize for a in args)
    size += sum(o.size * o.dtype.itemsize for o in outs)
    near = pl.BlockSpec(memory_space=pltpu.VMEM)
    far = pl.BlockSpec(memory_space=pl.ANY)
    return pl.pallas_call(
        body,
        out_shape=tuple(outs),
        in_specs=[far if k in far_in else near for k in range(len(args))],
        out_specs=tuple([near] * len(outs)),
        scratch_shapes=list(scratch),
        compiler_params=pltpu.CompilerParams(vmem_limit_bytes=grant),
        cost_estimate=pl.CostEstimate(flops=flops, bytes_accessed=size, transcendentals=0),
    )(*args)


def dot(a, b, dims):
    return lax.dot_general(a, b, dims, preferred_element_type=F32)


def norm_parts(values):
    row_mean = jnp.mean(values, axis=-1, keepdims=True)
    centred = values - row_mean
    variance = jnp.mean(centred * centred, axis=-1, keepdims=True)
    inverse = lax.rsqrt(variance + epsilon)
    return centred * inverse, inverse


def norm_backward(grad_normed, normed, inverse):
    mean_grad = jnp.mean(grad_normed, axis=-1, keepdims=True)
    mean_cross = jnp.mean(grad_normed * normed, axis=-1, keepdims=True)
    return inverse * (grad_normed - mean_grad - normed * mean_cross)


def gelu_both(pre_act):
    inner_arg = gelu_coeff * (pre_act + 0.044715 * pre_act * pre_act * pre_act)
    tangent = jnp.tanh(inner_arg)
    gelu_value = 0.5 * pre_act * (1.0 + tangent)
    gelu_slope = 0.5 * (1.0 + tangent) + 0.5 * pre_act * (1.0 - tangent * tangent) * gelu_coeff * (
        1.0 + 3.0 * 0.044715 * pre_act * pre_act
    )
    return gelu_value, gelu_slope


def column_of(row_ref):
    count = row_ref.shape[1]
    spread = jnp.broadcast_to(row_ref[...], (count, count))
    down = lax.broadcasted_iota(jnp.int32, (count, count), 0)
    along = lax.broadcasted_iota(jnp.int32, (count, count), 1)
    return jnp.sum(jnp.where(down == along, spread, 0), axis=1, keepdims=True)


def prepare(
    hidden_hbm, gain_hbm, image_hbm, id_hbm, out_ref, hidden_ref, gain_ref, image_ref, id_ref, sems
):
    width = hidden_ref.shape[1]
    arrays = ((hidden_hbm, hidden_ref), (gain_hbm, gain_ref), (image_hbm, image_ref), (id_hbm, id_ref))
    moves = [pltpu.make_async_copy(src, dst, sems.at[k]) for k, (src, dst) in enumerate(arrays)]
    for move in moves:
        move.start()
    moves[0].wait()
    normed, _ = norm_parts(hidden_ref[...].astype(F32))
    moves[1].wait()
    out_ref[:, :width] = (normed * gain_ref[...].reshape(1, width)).astype(BF16)
    moves[2].wait()
    moves[3].wait()
    image = image_ref[...].astype(F32)
    scale = lax.rsqrt(jnp.sum(image * image, axis=-1, keepdims=True) + epsilon)
    out_ref[:, width : 2 * width] = (image * scale).astype(BF16)
    ids = column_of(id_ref)
    lane = lax.broadcasted_iota(jnp.int32, (image.shape[0], LANES), 1)
    low = jnp.where(lane == 0, ids & 127, 0)
    high = jnp.where(lane == 1, ids >> 7, 0)
    out_ref[:, 2 * width :] = (low + high).astype(F32).astype(BF16)


def split(both_ref, rows_ref, image_ref):
    width = rows_ref.shape[2]
    rows_ref[...] = both_ref[:, :, :width]
    image_ref[...] = both_ref[:, :, width:]


def targets(image_ref, teacher_ref, id_ref, target_ref):
    sides, _, rows, deep = image_ref.shape
    group = sides * sides * rows
    marks = image_ref[:, :, :, deep - LANES :].reshape(group, LANES)
    row = lax.broadcasted_iota(jnp.int32, (8, LANES), 0)
    lane = lax.broadcasted_iota(jnp.int32, (8, LANES), 1)
    pick = jnp.where(row == lane, 1.0, 0.0).astype(BF16)
    ids = dot(pick, marks, NT)
    image_id = ids[0:1] + 128.0 * ids[1:2]
    text_id = column_of(id_ref).astype(F32)
    same = jnp.where(text_id == image_id, 0.5, 0.0)
    down = lax.broadcasted_iota(jnp.int32, (group, group), 0)
    along = lax.broadcasted_iota(jnp.int32, (1, group), 1)
    block = along // rows
    wanted = (lax.rem(block, sides) * sides + block // sides) * rows + lax.rem(along, rows)
    order = jnp.where(down == wanted, 1.0, 0.0).astype(BF16)
    teacher = dot(teacher_ref[...], order, NN)
    target_ref[...] = same + 0.5 * jax.nn.sigmoid(teacher)


def forward(all_ref, w_in_ref, w_out_ref, part_ref):
    blocks, rows, width = part_ref.shape
    pre_act = dot(all_ref[...].reshape(blocks * rows, width), w_in_ref[...], NT)
    value, _ = gelu_both(pre_act)
    part = dot(value.astype(BF16), w_out_ref[...], NN).astype(BF16)
    part_ref[...] = part.reshape(blocks, rows, width)


def middle(part_ref, hidden_ref, gain_ref, image_ref, target_ref, out_ref, grad_ref):
    blocks, rows, width = part_ref.shape
    total = part_ref[0].astype(F32)
    for k in range(1, blocks):
        total = total + part_ref[k].astype(F32)
    residual = hidden_ref[...].astype(F32) + total
    gain = gain_ref[...].reshape(1, width)
    normed, inverse = norm_parts(residual)
    final = normed * gain
    length = jnp.sqrt(jnp.sum(final * final, axis=-1, keepdims=True) + epsilon)
    unit = final / length
    images = image_ref[:, :, :, :width].reshape(blocks * rows, width)
    logits = dot(unit.astype(BF16), images, NT) * logit_scale + logit_bias
    pair_grad = (jax.nn.sigmoid(logits) - target_ref[...]).astype(BF16)
    text_grad = logit_scale * dot(pair_grad, images, NN)
    radial = jnp.sum(unit * text_grad, axis=-1, keepdims=True)
    grad_final = (text_grad - unit * radial) / length
    grad = norm_backward(grad_final * gain, normed, inverse)
    grad_ref[...] = grad
    sent = grad.astype(BF16)
    for k in range(blocks):
        out_ref[k] = sent


def backward(all_ref, w_in_ref, rows_ref, w_out_ref, grad_ref, act_ref, give_ref):
    blocks, rows, width = rows_ref.shape
    group = blocks * rows
    pre_act = dot(all_ref[...].reshape(group, width), w_in_ref[...], NT)
    value, slope = gelu_both(pre_act)
    act_ref[...] = value.astype(BF16)
    grad_act = dot(rows_ref[...].reshape(group, width), w_out_ref[...], NT)
    grad_ref[...] = (grad_act * slope).astype(BF16)
    weight_grad(1, act_ref, rows_ref, grad_ref, all_ref, give_ref)


def input_grad(grad_ref, w_in_ref, k0, k1, k2, k3, held):
    at = lax.axis_index("x")
    held[...] = dot(grad_ref[...], w_in_ref[...], NN).astype(BF16).reshape(held.shape)
    for k, out in enumerate((k0, k1, k2, k3)):
        x = lax.rem(at + k, 4)
        for z in range(4):
            out[z] = held[x * 4 + z]


def packed(a_ref, b_ref, out_ref):
    a = a_ref[...]
    units = a.shape[1]
    width = b_ref.shape[-1]
    blocks = width // LANES
    even = units // 8 * 8
    odd = units - even
    full = dot(a, b_ref[...].reshape(a.shape[0], width), TN).astype(out_ref.dtype)
    for c in range(blocks):
        tile = full[:, c * LANES : (c + 1) * LANES]
        out_ref[c * even : (c + 1) * even, :] = tile[:even]
        if odd:
            out_ref[blocks * even + c * odd : blocks * even + (c + 1) * odd, :] = tile[even:]


def weight_grad(first, act_ref, grads_ref, pre_ref, rows_ref, out_ref):
    units = act_ref.shape[1]
    width = grads_ref.shape[-1]
    core = lax.axis_index("co")
    used = units * (width // LANES) // 8 * 8
    tall = out_ref.shape[0]
    if used < tall:
        out_ref[used:tall, :] = jnp.zeros((tall - used, LANES), out_ref.dtype)

    @pl.when(core == first)
    def _():
        packed(act_ref, grads_ref, out_ref)

    @pl.when(core != first)
    def _():
        packed(pre_ref, rows_ref, out_ref)


def join(kept_ref, got_ref, out_ref):
    ring, chunk, lanes = out_ref.shape
    total = kept_ref[...] + got_ref[...].astype(F32)
    out_ref[...] = total.astype(BF16).reshape(ring, chunk, lanes)


def ring_sum(slices_ref, out_ref):
    total = slices_ref[0].astype(F32)
    for k in range(1, slices_ref.shape[0]):
        total = total + slices_ref[k].astype(F32)
    sent = total.astype(BF16)
    for k in range(out_ref.shape[0]):
        out_ref[k] = sent


def unpack(owner, src_ref, *refs):
    w_out_hbm, w_in_hbm, full_ref, sem = refs[-4:]
    units, width = full_ref.shape
    core = lax.axis_index("co")
    blocks = width // LANES
    even = units // 8 * 8
    odd = units - even
    for c in range(blocks):
        lanes = slice(c * LANES, (c + 1) * LANES)
        full_ref[:even, lanes] = src_ref[c * even : (c + 1) * even, :].astype(F32)
        if odd:
            at = blocks * even + c * odd
            full_ref[even:, lanes] = src_ref[at : at + odd, :].astype(F32)

    @pl.when(core == owner)
    def _():
        move = pltpu.make_async_copy(full_ref, w_out_hbm, sem)
        move.start()
        move.wait()

    @pl.when(core != owner)
    def _():
        move = pltpu.make_async_copy(full_ref, w_in_hbm, sem)
        move.start()
        move.wait()


def column_sum(k0, k1, k2, k3, keep_ref, s1, s2, s3, held):
    at = lax.axis_index("zh")
    total = k0[...].astype(F32) + k1[...].astype(F32)
    held[...] = total + k2[...].astype(F32) + k3[...].astype(F32)
    keep_ref[...] = held[at]
    for k, out in enumerate((s1, s2, s3)):
        out[...] = held[lax.rem(at + k + 1, 4)].astype(BF16)


def last(keep_ref, g1, g2, g3, hidden_ref, gain_ref, grad_ref, out_ref):
    total = keep_ref[...] + g1[...].astype(F32) + g2[...].astype(F32) + g3[...].astype(F32)
    normed, inverse = norm_parts(hidden_ref[...].astype(F32))
    out_ref[...] = grad_ref[...] + norm_backward(total * gain_ref[...].reshape(1, -1), normed, inverse)


def shift(value, axis, by):
    length = lax.axis_size(axis)
    return lax.ppermute(value, axis, [(i, (i + by) % length) for i in range(length)])


def unpack_call(owner, src, whole, units, width):
    far = pl.BlockSpec(memory_space=pl.ANY)
    near = pl.BlockSpec(memory_space=pltpu.VMEM)
    return pl.pallas_call(
        lambda *refs: unpack(owner, *refs),
        out_shape=(shape((units, width), F32),) * 2,
        in_specs=[near] + [far] * len(whole),
        out_specs=(far, far),
        scratch_shapes=[pltpu.VMEM((units, width), F32), pltpu.SemaphoreType.DMA(())],
        input_output_aliases={k + 1: k for k in range(len(whole))},
        compiler_params=pltpu.CompilerParams(vmem_limit_bytes=VMEM_GRANT),
        cost_estimate=pl.CostEstimate(
            flops=0, bytes_accessed=6 * units * width, transcendentals=0
        ),
    )(src, *whole)


def per_device(
    hidden_in, gain_mlp, gain_final, w_in, w_out, image_embeds, pair_ids, teacher_logits
):
    rows, width = hidden_in.shape
    units = w_in.shape[1]
    blocks = lax.axis_size(BLK)
    ring = lax.axis_size(RING)
    group = rows * blocks
    ids = pair_ids.reshape(1, rows)
    w_in_rows = w_in.T
    teacher = teacher_logits[0].T
    spread = shape((blocks, rows, width), BF16)
    matmul = 2 * group * units * width

    (own_rows,) = call(
        prepare,
        [shape((rows, 2 * width + LANES), BF16)],
        hidden_in,
        gain_mlp,
        image_embeds,
        ids,
        far_in=(0, 1, 2, 3),
        scratch=[
            pltpu.VMEM(hidden_in.shape, BF16),
            pltpu.VMEM(gain_mlp.shape, F32),
            pltpu.VMEM(image_embeds.shape, BF16),
            pltpu.VMEM(ids.shape, ids.dtype),
            pltpu.SemaphoreType.DMA((4,)),
        ],
        grant=WHOLE_GRANT,
    )
    both = lax.all_gather(own_rows, "zh")
    rows_column, column = call(
        split, [shape((4, rows, width), BF16), shape((4, rows, width + LANES), BF16)], both
    )
    group_input = lax.all_gather(rows_column, "x")
    (part,) = call(forward, [spread], group_input, w_in_rows, w_out, flops=2 * matmul)
    part, column = lax.optimization_barrier((part, column))
    images = lax.all_gather(column, "x")
    (target,) = call(targets, [shape((rows, group), F32)], images, teacher, ids)
    parts = lax.all_to_all(part, ARRIVAL, 0, 0)
    copies, grad_residual = call(
        middle, [spread, shape((rows, width), F32)], parts, hidden_in, gain_final, images, target
    )
    group_grads = lax.all_to_all(copies, ARRIVAL, 0, 0)
    chunk = -(-(units * (width // LANES)) // (8 * ring)) * 8
    tall = chunk * ring

    grad_pre, act, give = call(
        backward,
        [shape((group, units), BF16)] * 2 + [shape((tall, LANES), BF16)],
        group_input,
        w_in_rows,
        group_grads,
        w_out,
        flops=3 * matmul,
    )

    def grads(first, dtype):
        return call(
            lambda *refs: weight_grad(first, *refs),
            [shape((tall, LANES), dtype)],
            act,
            group_grads,
            grad_pre,
            group_input,
            flops=matmul,
        )[0]

    got = shift(give, "co", 1)
    keep = grads(0, F32)
    (mine,) = call(join, [shape((ring, chunk, LANES), BF16)], keep, got)
    slices = lax.all_to_all(mine, RING, 0, 0)

    quarter = shape((4, rows, width), BF16)
    k0, s1, s2, s3 = call(
        input_grad,
        [quarter] * 4,
        grad_pre,
        w_in_rows,
        flops=matmul,
        scratch=[pltpu.VMEM((blocks, rows, width), BF16)],
    )
    arrived = []
    for k, sent in ((1, s1), (2, s2), (3, s3)):
        arrived.append(shift(sent, "x", k))
    own, s1, s2, s3 = call(
        column_sum,
        [shape((rows, width), F32)] + [shape((rows, width), BF16)] * 3,
        k0,
        *arrived,
        scratch=[pltpu.VMEM((4, rows, width), F32)],
    )
    arrived = []
    for k, sent in ((1, s1), (2, s2), (3, s3)):
        arrived.append(shift(sent, "zh", k))
    (grad_hidden,) = call(
        last, [shape((rows, width), F32)], own, *arrived, hidden_in, gain_mlp, grad_residual
    )

    (copies,) = call(ring_sum, [shape((ring, chunk, LANES), BF16)], slices)
    whole = lax.all_to_all(copies, RING, 0, 0).reshape(tall, LANES)
    other = shift(whole, "co", 1)
    grad_w_out, grad_w_in = unpack_call(0, whole, (), units, width)
    grad_w_out, grad_w_in = unpack_call(1, other, (grad_w_out, grad_w_in), units, width)
    return (grad_hidden, grad_w_in.T, grad_w_out)


def solution(mesh):
    fine = Mesh(mesh.devices.reshape(2, 8, 2, 4, 4), ("zl", "y", "co", "zh", "x"))
    every = DP + BLK
    in_specs = (
        P(every, None),
        P(),
        P(),
        P(None, BLK),
        P(BLK, None),
        P(every, None),
        P(every),
        P(DP, None, BLK),
    )
    out_specs = (P(every, None), P(None, BLK), P(BLK, None))
    return jax.shard_map(
        per_device, mesh=fine, in_specs=in_specs, out_specs=out_specs, check_vma=False
    )
```
